32 devices in a mesh: dp: 4 (over y, x), expert: 8 (over z, core).
Axes of the slice: x: 2, y: 2, z: 4, core: 2. Of those that a mesh axis runs over, the one named last changes fastest.
Arguments:
- tokens: bfloat16 [4096, 1024], P(('dp', 'expert')), may hold values from -6 to 6
- cotangent: bfloat16 [4096, 1024], P(('dp', 'expert')), may hold values from -6 to 6
- gate_prob: float32 [4096], P(('dp', 'expert')), may hold values from 0.1 to 1
- bin_ids: int32 [4096, 1], P(('dp', 'expert')), may hold values from 0 to 7; in each aligned block of 128 rows (0 to 127, 128 to 255, ...) at most 48 rows name the same one
- w_gate: bfloat16 [8, 1024, 1408], P('expert', 'dp'), may hold values from -0.1875 to 0.1875
- w_up: bfloat16 [8, 1024, 1408], P('expert', 'dp'), may hold values from -0.1875 to 0.1875
- w_down: bfloat16 [8, 1408, 1024], P('expert', 'dp'), may hold values from -0.15625 to 0.15625
Outputs:
- d_tokens: bfloat16 [4096, 1024], P(('dp', 'expert'))
- d_gate: float32 [4096], P(('dp', 'expert'))
- d_w_down: float32 [8, 1408, 1024], P('expert', 'dp')
The draws below stay inside these ranges and needn't reach their ends.
Inputs may be any that keep to these rules, and one draw needn't show every extreme that they name: `bin_ids`: among the 128 rows of one device no bin is named more than 48 times, and on some devices some bin is named exactly 48 times.
All inputs are finite; a program needn't handle non-finite values.
Results may differ from the reference program's by a relative error of at most 0.014.
Values may be sent and summed in bfloat16 or wider, within the bound.
No kernel may reach another device: no remote copies, remote signals or barrier semaphores. Data moves between devices by JAX's collectives and lax.ppermute only.
A program may use at most 64 MiB of HBM per device.

```python
import math
import jax
import jax.numpy as jnp
import numpy as np
from jax import lax

D = 1024
FF = 1408
TOK_DEV = 128
EXPERTS = 8
CAP = 48
TOKENS = 4096
N_DP = 4


def steps_of(rng, shape, pieces, low, top_value):
    factor_of = 1.0
    for dim, blocks in pieces:
        draws = jax.random.uniform(jax.random.fold_in(jax.random.fold_in(rng, 6), dim), (blocks,), jnp.float32, low / len(pieces), top_value / len(pieces))
        factor_of = factor_of * jnp.repeat(jnp.exp(draws), shape[dim] // blocks).reshape((-1,) + (1,) * (len(shape) - 1 - dim))
    return factor_of


def shared_out(stream_key, own, number, rows, count, top, reach, skew):
    sequence = jax.random.permutation(stream_key, count)
    crowded, usual = shares(count, rows * top, reach, skew, True), shares(count, rows * top, reach, skew, False)
    places = jnp.arange(count)

    def named(sizes, rotation):
        used = int((sizes > 0).sum())
        fixed = max(1, used // 4)
        shifted = fixed + (places - fixed + rotation * (used - fixed)) % max(1, count - fixed)
        return jnp.zeros((count,), jnp.int32).at[sequence[jnp.where(places < fixed, places, shifted)]].set(jnp.asarray(sizes, jnp.int32))

    sizes = jnp.where(number % 4 == 0, named(crowded, number // 4), named(usual, number - number // 4 - 1))
    mixed = jax.random.permutation(jax.random.fold_in(own, 3), count)
    donor, sink = mixed[0:count // 2 * 2:2], mixed[1:count // 2 * 2:2]
    slack = jnp.minimum(sizes[donor] - 1, reach - sizes[sink]) // 2
    slack = jnp.where((donor == sequence[0]) | (sink == sequence[0]) | (sizes[sink] == 0), 0, jnp.maximum(slack, 0))
    shifted = jax.random.randint(jax.random.fold_in(own, 4), (count // 2,), 0, 1 << 20) % (slack + 1)
    sizes = sizes.at[donor].add(-shifted).at[sink].add(shifted)
    members = jnp.searchsorted(jnp.cumsum(sizes), jnp.arange(rows * top), side="right").astype(jnp.int32)
    grid = members.reshape(top, rows).T
    grid = grid[jax.random.permutation(jax.random.fold_in(own, 1), rows)]
    rotation = jax.random.randint(jax.random.fold_in(own, 2), (rows, 1), 0, top)
    return jnp.take_along_axis(grid, (jnp.arange(top)[None, :] + rotation) % top, axis=1)


def shares(amount, total, reach, slope, full):
    portions = [(1 << 20) // math.isqrt(standing ** slope) + 1 for standing in range(1, amount + 1)]
    largest = reach if full else min(reach, max(-(-total // amount), total * portions[0] // sum(portions)))
    least = 1 if total - largest >= amount - 1 else 0
    holding, spare = [largest] + [least] * (amount - 1), total - largest - least * (amount - 1)
    while spare > 0:
        free = [i for i in range(1, amount) if holding[i] < largest] or [i for i in range(1, amount) if holding[i] < reach]
        whole, budget = sum([portions[i] for i in free]), spare
        for i in free:
            extra = min(reach - holding[i], max(1, budget * portions[i] // whole), spare)
            holding[i] = holding[i] + extra
            spare = spare - extra
    return np.array(holding)


def bell_draw(rng, extent, width, most, split=(), kind=jnp.bfloat16):
    array = width * jax.random.normal(rng, extent, jnp.float32)
    if split:
        array = array * steps_of(rng, extent, split, -0.22, 0.18)
    return jnp.clip(array, -most, most).astype(kind)


def setup_inputs(seed: int = 0) -> dict:
    arg_keys = jax.random.split(jax.random.key(seed), 8)
    tokens = bell_draw(arg_keys[0], (TOKENS, D), 1.0, 6.0, ((0, 32),))
    cotangent = bell_draw(arg_keys[1], (TOKENS, D), 1.0, 6.0, ((0, 32),))
    gate_prob = jnp.clip(jnp.exp(math.log(1.0) - 2.3025851 * jax.random.uniform(arg_keys[2], (TOKENS,), jnp.float32) ** steps_of(arg_keys[2], (TOKENS,), ((0, 32),), -0.2, 0.2)), 0.1, 1.0)
    bin_ids_keys = jax.random.split(jax.random.fold_in(arg_keys[3], 1), TOKENS // TOK_DEV)
    bin_ids_turns = jax.random.permutation(jax.random.fold_in(arg_keys[3], 3), TOKENS // TOK_DEV)
    bin_ids = jax.vmap(lambda own, number: shared_out(jax.random.fold_in(arg_keys[3], 2), own, number, TOK_DEV, EXPERTS, 1, CAP, 2))(bin_ids_keys, bin_ids_turns).reshape((TOKENS, 1))
    w_gate = bell_draw(arg_keys[4], (EXPERTS, D, FF), D ** -0.5, 0.1875, ((0, 8), (1, 4)))
    w_up = bell_draw(arg_keys[5], (EXPERTS, D, FF), D ** -0.5, 0.1875, ((0, 8), (1, 4)))
    w_down = bell_draw(arg_keys[6], (EXPERTS, FF, D), FF ** -0.5, 0.15625, ((0, 8), (1, 4)))
    return {"tokens": tokens, "cotangent": cotangent, "gate_prob": gate_prob, "bin_ids": bin_ids, "w_gate": w_gate, "w_up": w_up, "w_down": w_down}


def assign_slots(ids_dev, experts, capacity):
    onehot = (ids_dev[:, None] == jnp.arange(experts, dtype=jnp.int32)[None, :]).astype(jnp.int32)
    before = jnp.cumsum(onehot, axis=0) - onehot
    position = jnp.sum(before * onehot, axis=1)
    return (ids_dev * capacity + position).astype(jnp.int32)


def expert_backward(inputs, upstream, scales, gate_w, up_w, down_w):
    gate_pre = jnp.dot(inputs, gate_w, preferred_element_type=jnp.float32)
    up_pre = jnp.dot(inputs, up_w, preferred_element_type=jnp.float32)
    sigmoid_g = jax.nn.sigmoid(gate_pre)
    silu_g = gate_pre * sigmoid_g
    hidden = (silu_g * up_pre).astype(jnp.bfloat16)
    down_back = lax.dot_general(upstream, down_w, (((1,), (1,)), ((), ())), preferred_element_type=jnp.float32)
    gate_slot = jnp.sum(hidden.astype(jnp.float32) * down_back, axis=1)
    hidden_back = scales[:, None] * down_back
    grad_gate = (hidden_back * up_pre * sigmoid_g * (1.0 + gate_pre * (1.0 - sigmoid_g))).astype(jnp.bfloat16)
    grad_up = (hidden_back * silu_g).astype(jnp.bfloat16)
    scaled = (scales[:, None] * upstream.astype(jnp.float32)).astype(jnp.bfloat16)
    input_back = lax.dot_general(grad_gate, gate_w, (((1,), (1,)), ((), ())), preferred_element_type=jnp.float32)
    input_back = input_back + lax.dot_general(grad_up, up_w, (((1,), (1,)), ((), ())), preferred_element_type=jnp.float32)
    weight_term = lax.dot_general(hidden, scaled, (((0,), (0,)), ((), ())), preferred_element_type=jnp.float32)
    return input_back.astype(jnp.bfloat16), gate_slot, weight_term


def reference(tokens, cotangent, gate_prob, bin_ids, w_gate, w_up, w_down):
    groups = N_DP
    experts = EXPERTS
    capacity = CAP
    per_dev = TOK_DEV
    inputs_all = tokens.reshape(groups, experts, per_dev, D)
    upstream_all = cotangent.reshape(groups, experts, per_dev, D)
    scales_all = gate_prob.reshape(groups, experts, per_dev)
    ids_all = bin_ids.reshape(groups, experts, per_dev).astype(jnp.int32)
    source = jnp.broadcast_to(jnp.arange(experts, dtype=jnp.int32)[:, None], (experts, per_dev))

    def group_step(total, packed):
        inputs_g, upstream_g, scales_g, ids_g = packed
        dest = jax.vmap(lambda row_ids: assign_slots(row_ids, experts, capacity))(ids_g)

        def dispatch(values, tail):
            buffer = jnp.zeros((experts, experts * capacity) + tail, values.dtype)
            buffer = buffer.at[source, dest].set(values)
            buffer = buffer.reshape((experts, experts, capacity) + tail)
            buffer = jnp.swapaxes(buffer, 0, 1)
            return buffer.reshape((experts, experts * capacity) + tail)

        sent_in = dispatch(inputs_g, (D,))
        sent_up = dispatch(upstream_g, (D,))
        sent_scale = dispatch(scales_g, ())

        def per_expert(items):
            return expert_backward(*items)

        back, gate_slot, terms = lax.map(per_expert, (sent_in, sent_up, sent_scale, w_gate, w_up, w_down))
        total = total + lax.optimization_barrier(terms.astype(jnp.bfloat16)).astype(jnp.float32)
        back = jnp.swapaxes(back.reshape(experts, experts, capacity, D), 0, 1).reshape(experts, experts * capacity, D)
        gate_slot = jnp.swapaxes(gate_slot.reshape(experts, experts, capacity), 0, 1).reshape(experts, experts * capacity)
        token_back = jnp.take_along_axis(back, dest[:, :, None], axis=1)
        gate_back = jnp.take_along_axis(gate_slot, dest, axis=1)
        return total, (token_back, gate_back)

    start = jnp.zeros((experts, FF, D), jnp.float32)
    total, (token_back, gate_back) = lax.scan(group_step, start, (inputs_all, upstream_all, scales_all, ids_all))
    return token_back.reshape(TOKENS, D), gate_back.reshape(TOKENS), total
```

```python
import jax
import jax.numpy as jnp
from jax import lax
from jax.sharding import PartitionSpec as P


def contract_last(left, right):
    return lax.dot_general(
        left, right, (((1,), (1,)), ((), ())), preferred_element_type=jnp.float32
    )


def dp_send(value, flip, dp):
    return lax.ppermute(value, "dp", [(i, i ^ flip) for i in range(dp)])


def gather_rows(shards, dp):
    if dp != 4:
        return [lax.all_gather(s, "dp", axis=0, tiled=True) for s in shards]
    near = [(dp_send(s, 1, dp), dp_send(s, 2, dp)) for s in shards]
    wholes = []
    me = lax.axis_index("dp")
    for own, (one, two) in zip(shards, near):
        rows = own.shape[0]
        half = rows // 2
        far_top = dp_send(one[:half], 2, dp)
        far_low = dp_send(two[half:], 1, dp)
        whole = jnp.zeros((dp * rows, own.shape[1]), own.dtype)
        for piece, flip, shift in (
            (own, 0, 0), (one, 1, 0), (two, 2, 0), (far_top, 3, 0), (far_low, 3, half)
        ):
            whole = lax.dynamic_update_slice(whole, piece, ((me ^ flip) * rows + shift, 0))
        wholes.append(whole)
    return wholes


def body(tokens, cotangent, gate_prob, bin_ids, w_gate, w_up, w_down):
    experts = lax.axis_size("expert")
    dp = lax.axis_size("dp")
    per_dev = tokens.shape[0]
    width = tokens.shape[1]
    capacity = 3 * per_dev // experts
    slots = experts * capacity
    route_ids = bin_ids[:, 0]
    onehot = (route_ids[:, None] == jnp.arange(experts, dtype=jnp.int32)[None, :]).astype(jnp.int32)
    before = jnp.cumsum(onehot, axis=0) - onehot
    dest = route_ids * capacity + jnp.sum(before * onehot, axis=1)
    scaled_rows = (gate_prob[:, None] * cotangent.astype(jnp.float32)).astype(jnp.bfloat16)

    def exchange(values):
        return lax.all_to_all(
            values.reshape(experts, capacity, width), "expert", split_axis=0, concat_axis=0, tiled=True
        ).reshape(slots, width)

    def dispatch(values):
        return exchange(jnp.zeros((slots, width), values.dtype).at[dest].set(values))

    whole_gate, whole_up = gather_rows([w_gate[0], w_up[0]], dp)
    inputs = dispatch(tokens)
    scaled = dispatch(scaled_rows)
    down_own, whole_gate, whole_up = lax.optimization_barrier((w_down[0], whole_gate, whole_up))
    (whole_down,) = gather_rows([down_own], dp)

    gate_pre = jnp.dot(inputs, whole_gate, preferred_element_type=jnp.float32)
    up_pre = jnp.dot(inputs, whole_up, preferred_element_type=jnp.float32)
    sigmoid_g = jax.nn.sigmoid(gate_pre)
    silu_g = gate_pre * sigmoid_g
    hidden = (silu_g * up_pre).astype(jnp.bfloat16)
    weight_term = lax.dot_general(
        hidden, scaled, (((0,), (0,)), ((), ())), preferred_element_type=jnp.float32
    ).astype(jnp.bfloat16)

    hidden_back = contract_last(scaled, whole_down)
    gate_slot = jnp.sum(hidden.astype(jnp.float32) * hidden_back, axis=1)
    grad_gate = (hidden_back * up_pre * sigmoid_g * (1.0 + gate_pre * (1.0 - sigmoid_g))).astype(
        jnp.bfloat16
    )
    grad_up = (hidden_back * silu_g).astype(jnp.bfloat16)
    input_back = (contract_last(grad_gate, whole_gate) + contract_last(grad_up, whole_up)).astype(
        jnp.bfloat16
    )
    all_gates = lax.all_gather(gate_slot, "expert", axis=0, tiled=False)
    back_rows = exchange(input_back)
    my = lax.axis_index("expert")
    own_gates = lax.dynamic_slice(all_gates, (0, my * capacity), (experts, capacity)).reshape(slots)
    d_tokens = jnp.take(back_rows, dest, axis=0)
    d_gate = jnp.take(own_gates, dest, axis=0) / gate_prob

    if dp == 4:
        me = lax.axis_index("dp")
        rows = weight_term.shape[0] // dp
        half = width // 2

        def part(flip, cols):
            return lax.dynamic_slice(
                weight_term, ((me ^ flip) * rows, cols * half), (rows, half)
            )

        left_far = dp_send(part(3, 0), 1, dp)
        left_near = dp_send(part(1, 0), 1, dp)
        right_far = dp_send(part(3, 1), 2, dp)
        right_near = dp_send(part(2, 1), 2, dp)
        f32 = jnp.float32
        left_on = (part(2, 0).astype(f32) + left_far.astype(f32)).astype(jnp.bfloat16)
        right_on = (part(1, 1).astype(f32) + right_far.astype(f32)).astype(jnp.bfloat16)
        left_last = dp_send(left_on, 2, dp)
        right_last = dp_send(right_on, 1, dp)
        left = part(0, 0).astype(f32) + left_near.astype(f32) + left_last.astype(f32)
        right = part(0, 1).astype(f32) + right_near.astype(f32) + right_last.astype(f32)
        grad_rows = jnp.concatenate([left, right], axis=1)
    else:
        grad_rows = lax.psum_scatter(
            weight_term, "dp", scatter_dimension=0, tiled=True
        ).astype(jnp.float32)
    return (d_tokens, d_gate, grad_rows[None])


def solution(mesh):
    placed = (
        P(("dp", "expert"), None),
        P(("dp", "expert"), None),
        P(("dp", "expert")),
        P(("dp", "expert"), None),
        P("expert", "dp", None),
        P("expert", "dp", None),
        P("expert", "dp", None),
    )
    return jax.shard_map(
        body,
        mesh=mesh,
        in_specs=placed,
        out_specs=(P(("dp", "expert"), None), P(("dp", "expert")), P("expert", "dp", None)),
        check_vma=False,
    )
```

```python
import functools

import jax
import jax.numpy as jnp
from jax import lax
from jax.experimental import pallas as pl
from jax.experimental.pallas import tpu as pltpu
from jax.sharding import PartitionSpec as P

F32 = jnp.float32
BF16 = jnp.bfloat16
LANES = 128
PARAMS = pltpu.CompilerParams(vmem_limit_bytes=40 << 20)
VMEM = pl.BlockSpec(memory_space=pltpu.VMEM)
SMEM = pl.BlockSpec(memory_space=pltpu.SMEM)


def like(shape, dtype):
    return jax.ShapeDtypeStruct(shape, dtype)


def call(kernel, n_scalar, n_in, outs, scratch=()):
    return pl.pallas_call(
        kernel,
        out_shape=outs,
        in_specs=[SMEM] * n_scalar + [VMEM] * n_in,
        out_specs=jax.tree.map(lambda _: VMEM, outs),
        scratch_shapes=list(scratch),
        compiler_params=PARAMS,
    )


def dot(left, right, dims):
    return lax.dot_general(left, right, ((dims[:1], dims[1:]), ((), ())), preferred_element_type=F32)


def eye(size):
    rows = lax.broadcasted_iota(jnp.int32, (size, size), 0)
    return rows == lax.broadcasted_iota(jnp.int32, (size, size), 1)


def to_column(row):
    size = row.shape[1]
    spread = jnp.broadcast_to(row, (size, size))
    return jnp.sum(jnp.where(eye(size), spread, jnp.zeros_like(spread)), axis=1, keepdims=True)


def to_row(column):
    size = column.shape[0]
    spread = jnp.broadcast_to(column, (size, size))
    return jnp.sum(jnp.where(eye(size), spread, jnp.zeros_like(spread)), axis=0, keepdims=True)


def dispatch_kernel(ids, prob, tokens, cotangent, dest, sent_in, sent_up, *, capacity):
    per_dev = tokens.shape[0]
    slots = sent_in.shape[0]
    id_row = ids[...]
    id_col = to_column(id_row)
    earlier = lax.broadcasted_iota(jnp.int32, (per_dev, per_dev), 0) < lax.broadcasted_iota(
        jnp.int32, (per_dev, per_dev), 1
    )
    same = jnp.where((id_col == id_row) & earlier, 1, 0)
    dest_row = id_row * capacity + jnp.sum(same, axis=0, keepdims=True)
    dest[...] = dest_row
    pick = jnp.where(
        lax.broadcasted_iota(jnp.int32, (slots, per_dev), 0) == dest_row, 1.0, 0.0
    ).astype(BF16)
    sent_in[...] = dot(pick, tokens[...], (1, 0)).astype(BF16)
    scaled = (to_column(prob[...]) * cotangent[...].astype(F32)).astype(BF16)
    sent_up[...] = dot(pick, scaled, (1, 0)).astype(BF16)


def halves_kernel(me, gate, up, mine, other, *, cols):
    rows = gate.shape[0]
    half = gate.shape[1] // 2
    first = me[0] // cols == 0
    for k, ref in enumerate((gate, up)):
        low = ref[:, :half]
        high = ref[:, half:]
        mine[k * rows:(k + 1) * rows, :] = jnp.where(first, low, high)
        other[k * rows:(k + 1) * rows, :] = jnp.where(first, high, low)


def piece_places(me, cols):
    row, col = me // cols, me % cols
    places = [row * cols + col, (1 - row) * cols + col]
    for k in range(1, cols):
        there = (col + cols - k) % cols
        places += [row * cols + there, (1 - row) * cols + there]
    return places


def forward_math(inputs, gate_w, up_w, hidden, slope, silu):
    gate_pre = dot(inputs, gate_w, (1, 0))
    up_pre = dot(inputs, up_w, (1, 0))
    sigmoid_g = jax.nn.sigmoid(gate_pre)
    silu_g = gate_pre * sigmoid_g
    hidden[...] = (silu_g * up_pre).astype(BF16)
    slope[...] = up_pre * sigmoid_g * (1.0 + gate_pre * (1.0 - sigmoid_g))
    silu[...] = silu_g


def forward_first_kernel(me, inputs, *refs, cols):
    pieces, (hidden, slope, silu, gate_w, up_w) = refs[:-5], refs[-5:]
    rows = pieces[0].shape[0] // 2
    for piece, place in zip(pieces, piece_places(me[0], cols)):
        at = pl.ds(pl.multiple_of(place * rows, rows), rows)
        gate_w[at, :] = piece[:rows, :]
        up_w[at, :] = piece[rows:, :]
    forward_math(inputs[...], gate_w[...], up_w[...], hidden, slope, silu)


def forward_kernel(inputs, gate_w, up_w, hidden, slope, silu):
    forward_math(inputs[...], gate_w[...], up_w[...], hidden, slope, silu)


def backward_kernel(me, scaled, hidden, slope, silu, gate_w, up_w, *refs, cols):
    pieces, (back, gate_slot, down_w) = refs[:-3], refs[-3:]
    rows = pieces[0].shape[0]
    col = me[0] % cols
    for k, piece in enumerate(pieces):
        there = (col + cols - k) % cols
        down_w[pl.ds(pl.multiple_of(there * rows, rows), rows), :] = piece[...]
    hidden_back = dot(scaled[...], down_w[...], (1, 1))
    slot_sums = jnp.sum(hidden[...].astype(F32) * hidden_back, axis=1, keepdims=True)
    for k in range(gate_slot.shape[0]):
        gate_slot[k:k + 1, :] = to_row(slot_sums[k * LANES:(k + 1) * LANES, :])
    grad_gate = (hidden_back * slope[...]).astype(BF16)
    grad_up = (hidden_back * silu[...]).astype(BF16)
    total = dot(grad_gate, gate_w[...], (1, 1)) + dot(grad_up, up_w[...], (1, 1))
    back[...] = total.astype(back.dtype)


def weight_kernel(me, hidden0, hidden1, scaled0, scaled1, kept, sent, term, *, cols):
    term[...] = dot(hidden0[...], scaled0[...], (0, 0)) + dot(hidden1[...], scaled1[...], (0, 0))
    rows = kept.shape[0]
    col = me[0] % cols
    kept[...] = term[pl.ds(pl.multiple_of(col * rows, rows), rows), :]
    for k in range(1, cols):
        there = (col + k) % cols
        sent[k - 1] = term[pl.ds(pl.multiple_of(there * rows, rows), rows), :].astype(BF16)


def return_kernel(dest, prob, gates, back, d_tokens, d_gate):
    per_dev = dest.shape[1]
    slots = back.shape[0]
    dest_row = dest[...]
    pick = jnp.where(
        lax.broadcasted_iota(jnp.int32, (slots, per_dev), 0) == dest_row, 1.0, 0.0
    ).astype(BF16)
    d_tokens[...] = dot(pick, back[...], (0, 0)).astype(BF16)
    dest_col = to_column(dest_row)
    total = jnp.zeros((per_dev, 1), F32)
    for k in range(gates.shape[0]):
        here = lax.broadcasted_iota(jnp.int32, (per_dev, LANES), 1) + k * LANES == dest_col
        row = jnp.broadcast_to(gates[k:k + 1, :], (per_dev, LANES))
        total = total + jnp.sum(jnp.where(here, row, 0.0), axis=1, keepdims=True)
    d_gate[...] = to_row(total) / prob[...]


def body(tokens, cotangent, gate_prob, bin_ids, w_gate, w_up, w_down):
    experts = lax.axis_size("expert")
    dp = lax.axis_size("dp")
    cols = dp // 2
    per_dev, width = tokens.shape
    ff = w_gate.shape[2]
    half = ff // 2
    gate_rows = w_gate.shape[1]
    down_rows = w_down.shape[1]
    capacity = 3 * per_dev // experts
    slots = experts * capacity
    me = lax.axis_index("dp").astype(jnp.int32).reshape(1)
    barrier = lax.optimization_barrier

    def over_rows(value):
        return lax.ppermute(value, "dp", [(i, (i + cols) % dp) for i in range(dp)])

    def over_cols(value, k):
        return lax.ppermute(
            value, "dp", [(i, i // cols * cols + (i + k) % cols) for i in range(dp)]
        )

    def exchange(values):
        tail = values.shape[1:]
        return lax.all_to_all(
            values.reshape((experts, slots // experts) + tail), "expert",
            split_axis=0, concat_axis=0, tiled=True,
        ).reshape((slots,) + tail)

    shifts = range(1, cols)
    prob_row = gate_prob.reshape(1, per_dev)
    mine, other = call(
        functools.partial(halves_kernel, cols=cols), 1, 2,
        (like((2 * gate_rows, half), BF16), like((2 * gate_rows, half), BF16)),
    )(me, w_gate[0], w_up[0])
    dest, sent_in, sent_up = call(
        functools.partial(dispatch_kernel, capacity=capacity), 0, 4,
        (like((1, per_dev), jnp.int32), like((slots, width), BF16), like((slots, width), BF16)),
    )(bin_ids.reshape(1, per_dev), prob_row, tokens, cotangent)

    across = over_rows(other)
    beside = [over_cols(mine, k) for k in shifts]
    in0 = exchange(sent_in)
    relayed = [over_cols(across, k) for k in shifts]
    down_own, _ = barrier((w_down[0], beside))
    downs = [down_own] + [over_cols(down_own, k) for k in shifts]
    sent_up, in0 = barrier((sent_up, in0))
    up0 = exchange(sent_up)
    in1 = over_rows(barrier((in0, across))[0])
    up1 = over_rows(barrier((up0, in1))[0])
    pieces = [mine, across] + [v for pair in zip(beside, relayed) for v in pair]

    acts = (like((slots, half), BF16), like((slots, half), F32), like((slots, half), F32))
    whole = like((width, half), BF16)
    hidden0, slope0, silu0, gate_w, up_w = call(
        functools.partial(forward_first_kernel, cols=cols), 1, 1 + dp, acts + (whole, whole)
    )(me, in0, *pieces)
    hidden1, slope1, silu1 = call(forward_kernel, 0, 3, acts)(in1, gate_w, up_w)

    def backward(scaled, hidden, slope, silu, kind):
        return call(
            functools.partial(backward_kernel, cols=cols), 1, 6 + cols,
            (like((slots, width), kind), like((slots // LANES, LANES), F32)),
            [pltpu.VMEM((half, width), BF16)],
        )(me, scaled, hidden, slope, silu, gate_w, up_w, *downs)

    back1, slot1 = backward(up1, hidden1, slope1, silu1, BF16)
    came = over_rows(back1)
    came_slot = over_rows(slot1)
    up0, _ = barrier((up0, back1))
    back0, slot0 = backward(up0, hidden0, slope0, silu0, F32)
    gates = exchange((slot0 + came_slot).reshape(slots, 1)).reshape(slots // LANES, LANES)
    kept, sent = call(
        functools.partial(weight_kernel, cols=cols), 1, 4,
        (like((down_rows, width), F32), like((cols - 1, down_rows, width), BF16)),
        [pltpu.VMEM((half, width), F32)],
    )(me, hidden0, hidden1, up0, up1)
    back = exchange((back0 + came.astype(F32)).astype(BF16))
    d_tokens, d_gate = call(
        return_kernel, 0, 4, (like((per_dev, width), BF16), like((1, per_dev), F32))
    )(dest, prob_row, gates, back)
    grad_rows = kept
    for k in shifts:
        grad_rows = grad_rows + over_cols(sent[k - 1], k).astype(F32)
    return (d_tokens, d_gate.reshape(per_dev), grad_rows[None])


def solution(mesh):
    placed = (
        P(("dp", "expert"), None),
        P(("dp", "expert"), None),
        P(("dp", "expert")),
        P(("dp", "expert"), None),
        P("expert", "dp", None),
        P("expert", "dp", None),
        P("expert", "dp", None),
    )
    return jax.shard_map(
        body,
        mesh=mesh,
        in_specs=placed,
        out_specs=(P(("dp", "expert"), None), P(("dp", "expert")), P("expert", "dp", None)),
        check_vma=False,
    )
```

```python
import functools

import jax
import jax.numpy as jnp
from jax import lax
from jax.experimental import pallas as pl
from jax.experimental.pallas import tpu as pltpu
from jax.sharding import PartitionSpec as P

F32 = jnp.float32
BF16 = jnp.bfloat16
LANES = 128
PARAMS = pltpu.CompilerParams(vmem_limit_bytes=40 << 20)
VMEM = pl.BlockSpec(memory_space=pltpu.VMEM)
SMEM = pl.BlockSpec(memory_space=pltpu.SMEM)


def like(shape, dtype):
    return jax.ShapeDtypeStruct(shape, dtype)


def call(kernel, n_scalar, n_in, outs, scratch=(), spec=VMEM):
    return pl.pallas_call(
        kernel,
        out_shape=outs,
        in_specs=[SMEM] * n_scalar + [spec] * n_in,
        out_specs=jax.tree.map(lambda _: VMEM, outs),
        scratch_shapes=list(scratch),
        compiler_params=PARAMS,
    )


def dot(left, right, dims):
    return lax.dot_general(left, right, ((dims[:1], dims[1:]), ((), ())), preferred_element_type=F32)


def eye(size):
    rows = lax.broadcasted_iota(jnp.int32, (size, size), 0)
    return rows == lax.broadcasted_iota(jnp.int32, (size, size), 1)


def to_column(row):
    size = row.shape[1]
    spread = jnp.broadcast_to(row, (size, size))
    return jnp.sum(jnp.where(eye(size), spread, jnp.zeros_like(spread)), axis=1, keepdims=True)


def to_row(column):
    size = column.shape[0]
    spread = jnp.broadcast_to(column, (size, size))
    return jnp.sum(jnp.where(eye(size), spread, jnp.zeros_like(spread)), axis=0, keepdims=True)


def dispatch_kernel(me, ids, prob, tokens, cotangent, dest, *blocks):
    per_dev = tokens.shape[0]
    capacity = blocks[0].shape[0] // 2
    slots = len(blocks) * capacity
    id_row = ids[...] ^ me[0]
    id_col = to_column(id_row)
    earlier = lax.broadcasted_iota(jnp.int32, (per_dev, per_dev), 0) < lax.broadcasted_iota(
        jnp.int32, (per_dev, per_dev), 1
    )
    same = jnp.where((id_col == id_row) & earlier, 1, 0)
    dest_row = id_row * capacity + jnp.sum(same, axis=0, keepdims=True)
    dest[...] = dest_row
    pick = jnp.where(
        lax.broadcasted_iota(jnp.int32, (slots, per_dev), 0) == dest_row, 1.0, 0.0
    ).astype(BF16)
    scaled = (to_column(prob[...]) * cotangent[...].astype(F32)).astype(BF16)
    for k, block in enumerate(blocks):
        rows = pick[k * capacity:(k + 1) * capacity, :]
        block[:capacity, :] = dot(rows, tokens[...], (1, 0)).astype(BF16)
        block[capacity:, :] = dot(rows, scaled, (1, 0)).astype(BF16)


def group_kernel(*refs):
    blocks, out = refs[:-1], refs[-1]
    capacity = blocks[0].shape[0] // 2
    tall = len(blocks) * capacity
    for k, block in enumerate(blocks):
        out[k * capacity:(k + 1) * capacity, :] = block[:capacity, :]
        out[tall + k * capacity:tall + (k + 1) * capacity, :] = block[capacity:, :]


def halves_kernel(me, gate, up, mine, other, *, cols):
    half = gate.shape[1] // 2
    first = me[0] // cols == 0
    for k, ref in enumerate((gate, up)):
        low = ref[:, :half]
        high = ref[:, half:]
        mine[:, k * half:(k + 1) * half] = jnp.where(first, low, high)
        other[:, k * half:(k + 1) * half] = jnp.where(first, high, low)


def piece_places(me, cols):
    row, col = me // cols, me % cols
    places = [row * cols + col, (1 - row) * cols + col]
    for k in range(1, cols):
        there = (col + cols - k) % cols
        places += [row * cols + there, (1 - row) * cols + there]
    return places


def forward_math(inputs, gate_w, up_w, hidden, slope, silu):
    gate_pre = dot(inputs, gate_w, (1, 0))
    up_pre = dot(inputs, up_w, (1, 0))
    sigmoid_g = jax.nn.sigmoid(gate_pre)
    silu_g = gate_pre * sigmoid_g
    hidden[...] = (silu_g * up_pre).astype(BF16)
    slope[...] = up_pre * sigmoid_g * (1.0 + gate_pre * (1.0 - sigmoid_g))
    silu[...] = silu_g


def token_rows(near, far):
    h = near.shape[0] // 2
    return jnp.concatenate([near[:h, :], far[:h, :]], axis=0)


def scaled_rows(near, far):
    h = near.shape[0] // 2
    return jnp.concatenate([near[h:, :], far[h:, :]], axis=0)


def forward_first_kernel(me, near, far, *refs, cols):
    pieces, (hidden, slope, silu, gate_w, up_w) = refs[:-5], refs[-5:]
    rows = pieces[0].shape[0]
    half = pieces[0].shape[1] // 2
    for piece, place in zip(pieces, piece_places(me[0], cols)):
        at = pl.ds(pl.multiple_of(place * rows, rows), rows)
        gate_w[at, :] = piece[:, :half]
        up_w[at, :] = piece[:, half:]
    forward_math(token_rows(near, far), gate_w[...], up_w[...], hidden, slope, silu)


def forward_kernel(near, far, gate_w, up_w, hidden, slope, silu):
    forward_math(token_rows(near, far), gate_w[...], up_w[...], hidden, slope, silu)


def backward_kernel(me, near, far, hidden, slope, silu, gate_w, up_w, *refs, cols):
    pieces, (back_near, back_far, down_w) = refs[:-3], refs[-3:]
    rows = pieces[0].shape[0]
    col = me[0] % cols
    for k, piece in enumerate(pieces):
        there = (col + cols - k) % cols
        down_w[pl.ds(pl.multiple_of(there * rows, rows), rows), :] = piece[...]
    hidden_back = dot(scaled_rows(near, far), down_w[...], (1, 1))
    slot_sums = jnp.sum(hidden[...].astype(F32) * hidden_back, axis=1, keepdims=True)
    grad_gate = (hidden_back * slope[...]).astype(BF16)
    grad_up = (hidden_back * silu[...]).astype(BF16)
    total = dot(grad_gate, gate_w[...], (1, 1)) + dot(grad_up, up_w[...], (1, 1))
    tall, width = back_near.shape[0], back_near.shape[1] - LANES
    for out, at in ((back_near, 0), (back_far, tall)):
        out[:, :width] = total[at:at + tall, :].astype(out.dtype)
        out[:, width:] = gate_lanes(slot_sums[at:at + tall, :], out.dtype)


def gate_lanes(column, kind):
    column = jnp.broadcast_to(column, (column.shape[0], LANES))
    lane = lax.broadcasted_iota(jnp.int32, column.shape, 1)
    top = column.astype(kind).astype(F32)
    return jnp.where(lane == 0, top, jnp.where(lane == 1, column - top, 0.0)).astype(kind)


def merge_kernel(own, came, *blocks):
    rows, width = blocks[0].shape[0], blocks[0].shape[1] - LANES
    for k, block in enumerate(blocks):
        total = own[k * rows:(k + 1) * rows, :] + came[k * rows:(k + 1) * rows, :].astype(F32)
        block[:, :width] = total[:, :width].astype(BF16)
        block[:, width:] = gate_lanes(jnp.sum(total[:, width:], axis=1, keepdims=True), BF16)


def weight_kernel(me, hidden0, hidden1, near0, far0, near1, far1, kept, sent, term, *, cols):
    term[...] = dot(hidden0[...], scaled_rows(near0, far0), (0, 0)) + dot(
        hidden1[...], scaled_rows(near1, far1), (0, 0)
    )
    rows = kept.shape[0]
    col = me[0] % cols
    kept[...] = term[pl.ds(pl.multiple_of(col * rows, rows), rows), :]
    for k in range(1, cols):
        there = (col + k) % cols
        sent[k - 1] = term[pl.ds(pl.multiple_of(there * rows, rows), rows), :].astype(BF16)


def return_kernel(dest, prob, *refs):
    blocks, (d_tokens, d_gate) = refs[:-2], refs[-2:]
    per_dev, width = d_tokens.shape
    back = jnp.concatenate([block[...] for block in blocks], axis=0)
    pick = jnp.where(
        lax.broadcasted_iota(jnp.int32, (back.shape[0], per_dev), 0) == dest[...], 1.0, 0.0
    ).astype(BF16)
    home = dot(pick, back, (0, 0))
    d_tokens[...] = home[:, :width].astype(BF16)
    d_gate[...] = to_row(jnp.sum(home[:, width:], axis=1, keepdims=True)) / prob[...]


def body(tokens, cotangent, gate_prob, bin_ids, w_gate, w_up, w_down):
    experts = lax.axis_size("expert")
    dp = lax.axis_size("dp")
    cols = dp // 2
    per_dev, width = tokens.shape
    ff = w_gate.shape[2]
    half = ff // 2
    gate_rows = w_gate.shape[1]
    down_rows = w_down.shape[1]
    capacity = 3 * per_dev // experts
    slots = experts * capacity
    here = experts // 2
    me = lax.axis_index("dp").astype(jnp.int32).reshape(1)
    my_expert = lax.axis_index("expert").astype(jnp.int32).reshape(1)

    def after(value, *done):
        return lax.optimization_barrier((value,) + done)[0]

    def over_rows(value):
        return lax.ppermute(value, "dp", [(i, (i + cols) % dp) for i in range(dp)])

    def over_cols(value, k):
        return lax.ppermute(
            value, "dp", [(i, i // cols * cols + (i + k) % cols) for i in range(dp)]
        )

    def flipped(value, k):
        return lax.ppermute(value, "expert", [(i, i ^ k) for i in range(experts)])

    shifts = range(1, cols)
    prob_row = gate_prob.reshape(1, per_dev)
    mine, other = call(
        functools.partial(halves_kernel, cols=cols), 1, 2,
        (like((gate_rows, ff), BF16), like((gate_rows, ff), BF16)), spec=pl.BlockSpec(),
    )(me, w_gate[0], w_up[0])
    dest, *blocks = call(
        dispatch_kernel, 1, 4,
        (like((1, per_dev), jnp.int32),) + (like((2 * capacity, width), BF16),) * experts,
        spec=pl.BlockSpec(),
    )(after(my_expert, mine), bin_ids.reshape(1, per_dev), prob_row, tokens, cotangent)

    across = over_rows(other)
    beside = [over_cols(mine, k) for k in shifts]
    came = {0: blocks[0]}

    def fetch(k, *done):
        came[k] = flipped(after(blocks[k], *done) if done else blocks[k], k)

    fetch(here)
    for k in range(2, here):
        fetch(k, *([came[k - 2]] if k >= 4 else []))
    fetch(here + 1, came[2])
    fetch(1, came[2], came[here])
    for k in range(here + 2, experts):
        fetch(k, came[k - 2])

    def group(flips):
        return call(group_kernel, 0, here, like((slots, width), BF16))(*[came[k] for k in flips])

    near0 = group(range(here))
    far0 = group(range(here, experts))
    near1 = over_rows(after(near0, across))
    far1 = over_rows(after(far0, near1))
    relayed = [over_cols(after(across, beside, came[here + 1]), k) for k in shifts]
    down_own = after(w_down[0], relayed, came[experts - 2])
    downs = [down_own] + [over_cols(down_own, k) for k in shifts]
    pieces = [mine, across] + [v for pair in zip(beside, relayed) for v in pair]

    acts = (like((slots, half), BF16), like((slots, half), F32), like((slots, half), F32))
    whole = like((width, half), BF16)
    hidden0, slope0, silu0, gate_w, up_w = call(
        functools.partial(forward_first_kernel, cols=cols), 1, 2 + dp, acts + (whole, whole)
    )(me, near0, far0, *pieces)
    hidden1, slope1, silu1 = call(forward_kernel, 0, 4, acts)(near1, far1, gate_w, up_w)

    def backward(near, far, hidden, slope, silu, kind):
        rows = like((slots // 2, width + LANES), kind)
        return call(
            functools.partial(backward_kernel, cols=cols), 1, 7 + cols,
            (rows, rows),
            [pltpu.VMEM((half, width), BF16)],
        )(me, near, far, hidden, slope, silu, gate_w, up_w, *downs)

    back_near1, back_far1 = backward(near1, far1, hidden1, slope1, silu1, BF16)
    came_far = over_rows(back_far1)
    came_near = over_rows(after(back_near1, came_far))
    back_near0, back_far0 = backward(
        after(near0, back_far1), far0, hidden0, slope0, silu0, F32
    )
    hidden0, _ = lax.optimization_barrier((hidden0, back_far0))
    kept, sent = call(
        functools.partial(weight_kernel, cols=cols), 1, 6,
        (like((down_rows, width), F32), like((cols - 1, down_rows, width), BF16)),
        [pltpu.VMEM((half, width), F32)],
    )(me, hidden0, hidden1, near0, far0, near1, far1)

    merge = call(merge_kernel, 0, 2, (like((capacity, width + LANES), BF16),) * here)
    far_blocks = merge(after(back_far0, sent), came_far)
    far_home = [flipped(b, here + k) for k, b in enumerate(far_blocks)]
    near_blocks = merge(back_near0, came_near)
    near_home = [near_blocks[0]] + [flipped(near_blocks[k], k) for k in range(1, here)]
    d_tokens, d_gate = call(
        return_kernel, 0, 2 + experts, (like((per_dev, width), BF16), like((1, per_dev), F32))
    )(dest, prob_row, *near_home, *far_home)
    grad_rows = kept
    for k in shifts:
        grad_rows = grad_rows + over_cols(sent[k - 1], k).astype(F32)
    return (d_tokens, d_gate.reshape(per_dev), grad_rows[None])


def solution(mesh):
    placed = (
        P(("dp", "expert"), None),
        P(("dp", "expert"), None),
        P(("dp", "expert")),
        P(("dp", "expert"), None),
        P("expert", "dp", None),
        P("expert", "dp", None),
        P("expert", "dp", None),
    )
    return jax.shard_map(
        body,
        mesh=mesh,
        in_specs=placed,
        out_specs=(P(("dp", "expert"), None), P(("dp", "expert")), P("expert", "dp", None)),
        check_vma=False,
    )
```

```python
import functools

import jax
import jax.numpy as jnp
from jax import lax
from jax.experimental import pallas as pl
from jax.experimental.pallas import tpu as pltpu
from jax.sharding import PartitionSpec as P

F32 = jnp.float32
BF16 = jnp.bfloat16
LANES = 128
PARAMS = pltpu.CompilerParams(vmem_limit_bytes=40 << 20)
VMEM = pl.BlockSpec(memory_space=pltpu.VMEM)
SMEM = pl.BlockSpec(memory_space=pltpu.SMEM)


def like(shape, dtype):
    return jax.ShapeDtypeStruct(shape, dtype)


def call(kernel, n_scalar, n_in, outs, scratch=(), spec=VMEM):
    return pl.pallas_call(
        kernel,
        out_shape=outs,
        in_specs=[SMEM] * n_scalar + [spec] * n_in,
        out_specs=jax.tree.map(lambda _: VMEM, outs),
        scratch_shapes=list(scratch),
        compiler_params=PARAMS,
    )


def dot(left, right, dims):
    return lax.dot_general(left, right, ((dims[:1], dims[1:]), ((), ())), preferred_element_type=F32)


def eye(size):
    rows = lax.broadcasted_iota(jnp.int32, (size, size), 0)
    return rows == lax.broadcasted_iota(jnp.int32, (size, size), 1)


def to_column(row):
    size = row.shape[1]
    spread = jnp.broadcast_to(row, (size, size))
    return jnp.sum(jnp.where(eye(size), spread, jnp.zeros_like(spread)), axis=1, keepdims=True)


def to_row(column):
    size = column.shape[0]
    spread = jnp.broadcast_to(column, (size, size))
    return jnp.sum(jnp.where(eye(size), spread, jnp.zeros_like(spread)), axis=0, keepdims=True)


def dispatch_kernel(me, ids, prob, tokens, cotangent, dest, *blocks):
    per_dev = tokens.shape[0]
    capacity = blocks[0].shape[0] // 2
    slots = len(blocks) * capacity
    id_row = ids[...] ^ me[0]
    id_col = to_column(id_row)
    earlier = lax.broadcasted_iota(jnp.int32, (per_dev, per_dev), 0) < lax.broadcasted_iota(
        jnp.int32, (per_dev, per_dev), 1
    )
    same = jnp.where((id_col == id_row) & earlier, 1, 0)
    dest_row = id_row * capacity + jnp.sum(same, axis=0, keepdims=True)
    dest[...] = dest_row
    pick = jnp.where(
        lax.broadcasted_iota(jnp.int32, (slots, per_dev), 0) == dest_row, 1.0, 0.0
    ).astype(BF16)
    scaled = (to_column(prob[...]) * cotangent[...].astype(F32)).astype(BF16)
    for k, block in enumerate(blocks):
        rows = pick[k * capacity:(k + 1) * capacity, :]
        block[:capacity, :] = dot(rows, tokens[...], (1, 0)).astype(BF16)
        block[capacity:, :] = dot(rows, scaled, (1, 0)).astype(BF16)


def group_kernel(*refs):
    blocks, out = refs[:-1], refs[-1]
    capacity = blocks[0].shape[0] // 2
    tall = len(blocks) * capacity
    for k, block in enumerate(blocks):
        out[k * capacity:(k + 1) * capacity, :] = block[:capacity, :]
        out[tall + k * capacity:tall + (k + 1) * capacity, :] = block[capacity:, :]


def halves_kernel(me, gate, up, mine, other, held, done, *, cols):
    copies = [
        pltpu.make_async_copy(ref, held.at[k], done.at[k]) for k, ref in enumerate((gate, up))
    ]
    for copy in copies:
        copy.start()
    half = gate.shape[1] // 2
    first = me[0] // cols == 0
    for k, copy in enumerate(copies):
        copy.wait()
        low = held[k, :, :half]
        high = held[k, :, half:]
        mine[:, k * half:(k + 1) * half] = jnp.where(first, low, high)
        other[:, k * half:(k + 1) * half] = jnp.where(first, high, low)


def piece_places(me, cols):
    row, col = me // cols, me % cols
    places = [row * cols + col, (1 - row) * cols + col]
    for k in range(1, cols):
        there = (col + cols - k) % cols
        places += [row * cols + there, (1 - row) * cols + there]
    return places


def forward_math(inputs, gate_w, up_w, hidden, slope, silu):
    gate_pre = dot(inputs, gate_w, (1, 0))
    up_pre = dot(inputs, up_w, (1, 0))
    sigmoid_g = jax.nn.sigmoid(gate_pre)
    silu_g = gate_pre * sigmoid_g
    hidden[...] = (silu_g * up_pre).astype(BF16)
    slope[...] = up_pre * sigmoid_g * (1.0 + gate_pre * (1.0 - sigmoid_g))
    silu[...] = silu_g


def token_rows(parts):
    return jnp.concatenate([p[:p.shape[0] // 2, :] for p in parts], axis=0)


def scaled_rows(parts):
    return jnp.concatenate([p[p.shape[0] // 2:, :] for p in parts], axis=0)


def forward_first_kernel(me, part, *refs, cols):
    pieces, (hidden, slope, silu, gate_w, up_w) = refs[:-5], refs[-5:]
    rows = pieces[0].shape[0]
    half = pieces[0].shape[1] // 2
    for piece, place in zip(pieces, piece_places(me[0], cols)):
        at = pl.ds(pl.multiple_of(place * rows, rows), rows)
        gate_w[at, :] = piece[:, :half]
        up_w[at, :] = piece[:, half:]
    forward_math(token_rows([part]), gate_w[...], up_w[...], hidden, slope, silu)


def forward_kernel(part, gate_w, up_w, hidden, slope, silu):
    forward_math(token_rows([part]), gate_w[...], up_w[...], hidden, slope, silu)


def down_kernel(me, *refs, cols):
    pieces, down_w = refs[:-1], refs[-1]
    rows = pieces[0].shape[0]
    for k, piece in enumerate(pieces):
        there = (me[0] % cols + cols - k) % cols
        down_w[pl.ds(pl.multiple_of(there * rows, rows), rows), :] = piece[...]


def backward_kernel(hidden, slope, silu, gate_w, up_w, down_w, part, back):
    hidden_back = dot(scaled_rows([part]), down_w[...], (1, 1))
    slot_sums = jnp.sum(hidden[...].astype(F32) * hidden_back, axis=1, keepdims=True)
    grad_gate = (hidden_back * slope[...]).astype(BF16)
    grad_up = (hidden_back * silu[...]).astype(BF16)
    width = back.shape[1] - LANES
    back[:, :width] = (
        dot(grad_gate, gate_w[...], (1, 1)) + dot(grad_up, up_w[...], (1, 1))
    ).astype(back.dtype)
    back[:, width:] = gate_lanes(slot_sums, back.dtype)


def gate_lanes(column, kind):
    column = jnp.broadcast_to(column, (column.shape[0], LANES))
    lane = lax.broadcasted_iota(jnp.int32, column.shape, 1)
    top = column.astype(kind).astype(F32)
    return jnp.where(lane == 0, top, jnp.where(lane == 1, column - top, 0.0)).astype(kind)


def merge_kernel(own, came, *blocks):
    rows, width = blocks[0].shape[0], blocks[0].shape[1] - LANES
    for k, block in enumerate(blocks):
        total = own[k * rows:(k + 1) * rows, :] + came[k * rows:(k + 1) * rows, :].astype(F32)
        block[:, :width] = total[:, :width].astype(BF16)
        block[:, width:] = gate_lanes(jnp.sum(total[:, width:], axis=1, keepdims=True), BF16)


def weight_kernel(me, *refs, cols, n_hidden):
    hiddens, parts, (kept, sent, term) = refs[:n_hidden], refs[n_hidden:-3], refs[-3:]
    hidden = jnp.concatenate([h[...] for h in hiddens], axis=0)
    term[...] = dot(hidden, scaled_rows(parts), (0, 0))
    rows = kept.shape[0]
    col = me[0] % cols
    kept[...] = term[pl.ds(pl.multiple_of(col * rows, rows), rows), :]
    for k in range(1, cols):
        there = (col + k) % cols
        sent[k - 1] = term[pl.ds(pl.multiple_of(there * rows, rows), rows), :].astype(BF16)


def return_kernel(dest, prob, *refs):
    blocks, (d_tokens, d_gate) = refs[:-2], refs[-2:]
    per_dev, width = d_tokens.shape
    back = jnp.concatenate([block[...] for block in blocks], axis=0)
    pick = jnp.where(
        lax.broadcasted_iota(jnp.int32, (back.shape[0], per_dev), 0) == dest[...], 1.0, 0.0
    ).astype(BF16)
    home = dot(pick, back, (0, 0))
    d_tokens[...] = home[:, :width].astype(BF16)
    d_gate[...] = to_row(jnp.sum(home[:, width:], axis=1, keepdims=True)) / prob[...]


def body(tokens, cotangent, gate_prob, bin_ids, w_gate, w_up, w_down):
    experts = lax.axis_size("expert")
    dp = lax.axis_size("dp")
    cols = dp // 2
    per_dev, width = tokens.shape
    ff = w_gate.shape[2]
    half = ff // 2
    gate_rows = w_gate.shape[1]
    down_rows = w_down.shape[1]
    capacity = 3 * per_dev // experts
    slots = experts * capacity
    here = experts // 2
    me = lax.axis_index("dp").astype(jnp.int32).reshape(1)
    my_expert = lax.axis_index("expert").astype(jnp.int32).reshape(1)

    def after(value, *done):
        return lax.optimization_barrier((value,) + done)[0]

    def over_rows(value):
        return lax.ppermute(value, "dp", [(i, (i + cols) % dp) for i in range(dp)])

    def over_cols(value, k):
        return lax.ppermute(
            value, "dp", [(i, i // cols * cols + (i + k) % cols) for i in range(dp)]
        )

    def flipped(value, k):
        return lax.ppermute(value, "expert", [(i, i ^ k) for i in range(experts)])

    shifts = range(1, cols)
    prob_row = gate_prob.reshape(1, per_dev)
    mine, other = call(
        functools.partial(halves_kernel, cols=cols), 1, 2,
        (like((gate_rows, ff), BF16), like((gate_rows, ff), BF16)),
        [pltpu.VMEM((2, gate_rows, ff), BF16), pltpu.SemaphoreType.DMA((2,))],
        pl.BlockSpec(memory_space=pl.ANY),
    )(me, *[pltpu.with_memory_space_constraint(w[0], pltpu.HBM) for w in (w_gate, w_up)])
    dest, *blocks = call(
        dispatch_kernel, 1, 4,
        (like((1, per_dev), jnp.int32),) + (like((2 * capacity, width), BF16),) * experts,
        spec=pl.BlockSpec(),
    )(after(my_expert, mine), bin_ids.reshape(1, per_dev), prob_row, tokens, cotangent)

    across = over_rows(other)
    beside = [over_cols(mine, k) for k in shifts]
    came = {0: blocks[0]}

    def fetch(k, *done):
        came[k] = flipped(after(blocks[k], *done) if done else blocks[k], k)

    fetch(here)
    for k in range(2, here):
        fetch(k, *([came[k - 2]] if k >= 4 else []))
    fetch(here + 1, came[2])
    fetch(1, came[2], came[here])
    for k in range(here + 2, experts):
        fetch(k, came[k - 2])

    def group(flips):
        return call(group_kernel, 0, len(flips), like((2 * capacity * len(flips), width), BF16))(
            *[came[k] for k in flips]
        )

    middle = here + here // 2
    spans = (range(here), range(here, middle), range(middle, experts))
    parts0 = [group(span) for span in spans]
    near1 = over_rows(after(parts0[0], across))
    mid1 = over_rows(after(parts0[1], near1, came[experts - 2]))
    last1 = over_rows(after(parts0[2], mid1))
    relayed = [over_cols(after(across, beside), k) for k in shifts]
    down_own = after(w_down[0], relayed)
    downs = [down_own] + [over_cols(down_own, k) for k in shifts]
    pieces = [mine, across] + [v for pair in zip(beside, relayed) for v in pair]

    def acts(rows):
        return (like((rows, half), BF16), like((rows, half), F32), like((rows, half), F32))

    def tall(part):
        return part.shape[0] // 2

    whole = like((width, half), BF16)
    *first, gate_w, up_w = call(
        functools.partial(forward_first_kernel, cols=cols), 1, 1 + dp,
        acts(tall(parts0[0])) + (whole, whole),
    )(me, parts0[0], *pieces)
    down_w = call(
        functools.partial(down_kernel, cols=cols), 1, cols, like((half, width), BF16)
    )(me, *downs)

    def forward(part):
        return call(forward_kernel, 0, 3, acts(tall(part)))(part, gate_w, up_w)

    def backward(values, part, kind):
        return call(
            backward_kernel, 0, 7, like((tall(part), width + LANES), kind)
        )(*values, gate_w, up_w, down_w, part)

    def merge(own, came, n):
        return call(merge_kernel, 0, 2, (like((capacity, width + LANES), BF16),) * n)(own, came)

    near0, mid0, last0 = parts0
    acts0 = [first, forward(mid0), forward(last0)]
    acts1 = [forward(near1), forward(mid1)]
    ready = [values[0] for values in acts0 + acts1]
    back_mid1 = backward([after(acts1[1][0], *ready), *acts1[1][1:]], mid1, BF16)
    came_mid = over_rows(after(back_mid1, last1))
    acts1.append(forward(after(last1, back_mid1)))
    back_last1 = backward(acts1[2], last1, BF16)
    came_last = over_rows(after(back_last1, came_mid))
    back_mid0 = backward(acts0[1], after(mid0, back_last1), F32)
    kept, sent = call(
        functools.partial(weight_kernel, cols=cols, n_hidden=6), 1, 12,
        (like((down_rows, width), F32), like((cols - 1, down_rows, width), BF16)),
        [pltpu.VMEM((half, width), F32)],
    )(me, after(acts0[0][0], back_mid0), acts0[1][0], acts0[2][0], *[a[0] for a in acts1],
      near0, mid0, last0, near1, mid1, last1)
    back_near1 = backward(acts1[0], after(near1, kept), BF16)
    mid_blocks = merge(back_mid0, came_mid, middle - here)
    came_near = over_rows(after(back_near1, came_last, *mid_blocks))
    back_last0 = backward(acts0[2], after(last0, came_last), F32)
    last_blocks = merge(back_last0, came_last, experts - middle)
    back_near0 = backward(acts0[0], after(near0, *last_blocks), F32)
    grad_came = [over_cols(sent[k - 1], k) for k in shifts]
    home = {}
    for k, block in enumerate(mid_blocks + last_blocks):
        home[here + k] = flipped(block, here + k)
    near_blocks = merge(back_near0, came_near, here)
    home[0] = near_blocks[0]
    for k in range(1, here):
        home[k] = flipped(near_blocks[k], k)
    d_tokens, d_gate = call(
        return_kernel, 0, 2 + experts, (like((per_dev, width), BF16), like((1, per_dev), F32))
    )(dest, prob_row, *[home[k] for k in range(experts)])
    grad_rows = kept
    for value in grad_came:
        grad_rows = grad_rows + value.astype(F32)
    return (d_tokens, d_gate.reshape(per_dev), grad_rows[None])


def solution(mesh):
    placed = (
        P(("dp", "expert"), None),
        P(("dp", "expert"), None),
        P(("dp", "expert")),
        P(("dp", "expert"), None),
        P("expert", "dp", None),
        P("expert", "dp", None),
        P("expert", "dp", None),
    )
    return jax.shard_map(
        body,
        mesh=mesh,
        in_specs=placed,
        out_specs=(P(("dp", "expert"), None), P(("dp", "expert")), P("expert", "dp", None)),
        check_vma=False,
    )
```

```python
import functools

import jax
import jax.numpy as jnp
from jax import lax
from jax.experimental import pallas as pl
from jax.experimental.pallas import tpu as pltpu
from jax.sharding import PartitionSpec as P

F32 = jnp.float32
BF16 = jnp.bfloat16
LANES = 128
PARAMS = pltpu.CompilerParams(vmem_limit_bytes=40 << 20)
VMEM = pl.BlockSpec(memory_space=pltpu.VMEM)
SMEM = pl.BlockSpec(memory_space=pltpu.SMEM)


def like(shape, dtype):
    return jax.ShapeDtypeStruct(shape, dtype)


def call(kernel, n_scalar, n_in, outs, scratch=(), spec=VMEM):
    return pl.pallas_call(
        kernel,
        out_shape=outs,
        in_specs=[SMEM] * n_scalar + [spec] * n_in,
        out_specs=jax.tree.map(lambda _: VMEM, outs),
        scratch_shapes=list(scratch),
        compiler_params=PARAMS,
    )


def dot(left, right, dims):
    return lax.dot_general(left, right, ((dims[:1], dims[1:]), ((), ())), preferred_element_type=F32)


def eye(size):
    rows = lax.broadcasted_iota(jnp.int32, (size, size), 0)
    return rows == lax.broadcasted_iota(jnp.int32, (size, size), 1)


def to_column(row):
    size = row.shape[1]
    spread = jnp.broadcast_to(row, (size, size))
    return jnp.sum(jnp.where(eye(size), spread, jnp.zeros_like(spread)), axis=1, keepdims=True)


def to_row(column):
    size = column.shape[0]
    spread = jnp.broadcast_to(column, (size, size))
    return jnp.sum(jnp.where(eye(size), spread, jnp.zeros_like(spread)), axis=0, keepdims=True)


def dispatch_kernel(me, ids, prob, tokens, cotangent, dest, *blocks):
    per_dev = tokens.shape[0]
    capacity = blocks[0].shape[0] // 2
    slots = len(blocks) * capacity
    id_row = ids[...] ^ me[0]
    id_col = to_column(id_row)
    earlier = lax.broadcasted_iota(jnp.int32, (per_dev, per_dev), 0) < lax.broadcasted_iota(
        jnp.int32, (per_dev, per_dev), 1
    )
    same = jnp.where((id_col == id_row) & earlier, 1, 0)
    dest_row = id_row * capacity + jnp.sum(same, axis=0, keepdims=True)
    dest[...] = dest_row
    pick = jnp.where(
        lax.broadcasted_iota(jnp.int32, (slots, per_dev), 0) == dest_row, 1.0, 0.0
    ).astype(BF16)
    scaled = (to_column(prob[...]) * cotangent[...].astype(F32)).astype(BF16)
    for k, block in enumerate(blocks):
        rows = pick[k * capacity:(k + 1) * capacity, :]
        block[:capacity, :] = dot(rows, tokens[...], (1, 0)).astype(BF16)
        block[capacity:, :] = dot(rows, scaled, (1, 0)).astype(BF16)


def group_kernel(*refs):
    blocks, out = refs[:-1], refs[-1]
    capacity = blocks[0].shape[0] // 2
    tall = len(blocks) * capacity
    for k, block in enumerate(blocks):
        out[k * capacity:(k + 1) * capacity, :] = block[:capacity, :]
        out[tall + k * capacity:tall + (k + 1) * capacity, :] = block[capacity:, :]


def halves_kernel(me, gate, up, mine, other, held, done, *, cols):
    copies = [
        pltpu.make_async_copy(ref, held.at[k], done.at[k]) for k, ref in enumerate((gate, up))
    ]
    for copy in copies:
        copy.start()
    half = gate.shape[1] // 2
    first = me[0] // cols == 0
    for k, copy in enumerate(copies):
        copy.wait()
        low = held[k, :, :half]
        high = held[k, :, half:]
        mine[:, k * half:(k + 1) * half] = jnp.where(first, low, high)
        other[:, k * half:(k + 1) * half] = jnp.where(first, high, low)


def piece_places(me, cols):
    row, col = me // cols, me % cols
    places = [row * cols + col, (1 - row) * cols + col]
    for k in range(1, cols):
        there = (col + cols - k) % cols
        places += [row * cols + there, (1 - row) * cols + there]
    return places


def forward_math(inputs, gate_w, up_w, hidden, slope, silu):
    gate_pre = dot(inputs, gate_w, (1, 0))
    up_pre = dot(inputs, up_w, (1, 0))
    sigmoid_g = jax.nn.sigmoid(gate_pre)
    silu_g = gate_pre * sigmoid_g
    hidden[...] = (silu_g * up_pre).astype(BF16)
    slope[...] = up_pre * sigmoid_g * (1.0 + gate_pre * (1.0 - sigmoid_g))
    silu[...] = silu_g


def token_rows(parts):
    return jnp.concatenate([p[:p.shape[0] // 2, :] for p in parts], axis=0)


def scaled_rows(parts):
    return jnp.concatenate([p[p.shape[0] // 2:, :] for p in parts], axis=0)


def forward_first_kernel(me, part, *refs, cols):
    pieces, (hidden, slope, silu, gate_w, up_w) = refs[:-5], refs[-5:]
    rows = pieces[0].shape[0]
    half = pieces[0].shape[1] // 2
    for piece, place in zip(pieces, piece_places(me[0], cols)):
        at = pl.ds(pl.multiple_of(place * rows, rows), rows)
        gate_w[at, :] = piece[:, :half]
        up_w[at, :] = piece[:, half:]
    forward_math(token_rows([part]), gate_w[...], up_w[...], hidden, slope, silu)


def forward_kernel(part, gate_w, up_w, hidden, slope, silu):
    forward_math(token_rows([part]), gate_w[...], up_w[...], hidden, slope, silu)


def down_kernel(me, *refs, cols):
    pieces, down_w = refs[:-1], refs[-1]
    rows = pieces[0].shape[0]
    for k, piece in enumerate(pieces):
        there = (me[0] % cols + cols - k) % cols
        down_w[pl.ds(pl.multiple_of(there * rows, rows), rows), :] = piece[...]


def backward_kernel(gate_w, up_w, down_w, *refs):
    n = len(refs) // 4
    hidden, slope, silu = (
        jnp.concatenate([r[...] for r in refs[k * n:(k + 1) * n]], axis=0) for k in range(3)
    )
    parts, back = refs[3 * n:4 * n], refs[-1]
    hidden_back = dot(scaled_rows(parts), down_w[...], (1, 1))
    slot_sums = jnp.sum(hidden.astype(F32) * hidden_back, axis=1, keepdims=True)
    grad_gate = (hidden_back * slope).astype(BF16)
    grad_up = (hidden_back * silu).astype(BF16)
    width = back.shape[1] - LANES
    back[:, :width] = (
        dot(grad_gate, gate_w[...], (1, 1)) + dot(grad_up, up_w[...], (1, 1))
    ).astype(back.dtype)
    back[:, width:] = gate_lanes(slot_sums, back.dtype)


def gate_lanes(column, kind):
    column = jnp.broadcast_to(column, (column.shape[0], LANES))
    lane = lax.broadcasted_iota(jnp.int32, column.shape, 1)
    top = column.astype(kind).astype(F32)
    return jnp.where(lane == 0, top, jnp.where(lane == 1, column - top, 0.0)).astype(kind)


def merge_kernel(own, came, *blocks):
    rows, width = blocks[0].shape[0], blocks[0].shape[1] - LANES
    for k, block in enumerate(blocks):
        total = own[k * rows:(k + 1) * rows, :] + came[k * rows:(k + 1) * rows, :].astype(F32)
        block[:, :width] = total[:, :width].astype(BF16)
        block[:, width:] = gate_lanes(jnp.sum(total[:, width:], axis=1, keepdims=True), BF16)


def weight_kernel(me, *refs, cols, n_hidden):
    hiddens, parts, (kept, sent, term) = refs[:n_hidden], refs[n_hidden:-3], refs[-3:]
    hidden = jnp.concatenate([h[...] for h in hiddens], axis=0)
    term[...] = dot(hidden, scaled_rows(parts), (0, 0))
    rows = kept.shape[0]
    col = me[0] % cols
    kept[...] = term[pl.ds(pl.multiple_of(col * rows, rows), rows), :]
    for k in range(1, cols):
        there = (col + k) % cols
        sent[k - 1] = term[pl.ds(pl.multiple_of(there * rows, rows), rows), :].astype(BF16)


def return_kernel(dest, prob, *refs):
    blocks, (d_tokens, d_gate) = refs[:-2], refs[-2:]
    per_dev, width = d_tokens.shape
    back = jnp.concatenate([block[...] for block in blocks], axis=0)
    pick = jnp.where(
        lax.broadcasted_iota(jnp.int32, (back.shape[0], per_dev), 0) == dest[...], 1.0, 0.0
    ).astype(BF16)
    home = dot(pick, back, (0, 0))
    d_tokens[...] = home[:, :width].astype(BF16)
    d_gate[...] = to_row(jnp.sum(home[:, width:], axis=1, keepdims=True)) / prob[...]


def body(tokens, cotangent, gate_prob, bin_ids, w_gate, w_up, w_down):
    experts = lax.axis_size("expert")
    dp = lax.axis_size("dp")
    cols = dp // 2
    per_dev, width = tokens.shape
    ff = w_gate.shape[2]
    half = ff // 2
    gate_rows = w_gate.shape[1]
    down_rows = w_down.shape[1]
    capacity = 3 * per_dev // experts
    slots = experts * capacity
    here = experts // 2
    me = lax.axis_index("dp").astype(jnp.int32).reshape(1)
    my_expert = lax.axis_index("expert").astype(jnp.int32).reshape(1)

    def after(value, *done):
        return lax.optimization_barrier((value,) + done)[0]

    def over_rows(value):
        return lax.ppermute(value, "dp", [(i, (i + cols) % dp) for i in range(dp)])

    def over_cols(value, k):
        return lax.ppermute(
            value, "dp", [(i, i // cols * cols + (i + k) % cols) for i in range(dp)]
        )

    def flipped(value, k):
        return lax.ppermute(value, "expert", [(i, i ^ k) for i in range(experts)])

    shifts = range(1, cols)
    prob_row = gate_prob.reshape(1, per_dev)
    mine, other = call(
        functools.partial(halves_kernel, cols=cols), 1, 2,
        (like((gate_rows, ff), BF16), like((gate_rows, ff), BF16)),
        [pltpu.VMEM((2, gate_rows, ff), BF16), pltpu.SemaphoreType.DMA((2,))],
        pl.BlockSpec(memory_space=pl.ANY),
    )(me, *[pltpu.with_memory_space_constraint(w[0], pltpu.HBM) for w in (w_gate, w_up)])
    dest, *blocks = call(
        dispatch_kernel, 1, 4,
        (like((1, per_dev), jnp.int32),) + (like((2 * capacity, width), BF16),) * experts,
        spec=pl.BlockSpec(),
    )(after(my_expert, mine), bin_ids.reshape(1, per_dev), prob_row, tokens, cotangent)

    across = over_rows(other)
    beside = [over_cols(mine, k) for k in shifts]
    came = {0: blocks[0]}

    def fetch(k, *done):
        came[k] = flipped(after(blocks[k], *done) if done else blocks[k], k)

    fetch(here)
    for k in range(2, here):
        fetch(k, *([came[k - 2]] if k >= 4 else []))
    fetch(here + 1, came[2])
    fetch(1, came[2], came[here])
    for k in range(here + 2, experts):
        fetch(k, came[k - 2])

    def group(flips):
        return call(group_kernel, 0, len(flips), like((2 * capacity * len(flips), width), BF16))(
            *[came[k] for k in flips]
        )

    middle = here + here // 2
    spans = (range(here), range(here, middle), range(middle, experts))
    parts0 = [group(span) for span in spans]
    near1 = over_rows(after(parts0[0], across))
    mid1 = over_rows(after(parts0[1], near1, came[experts - 2]))
    last1 = over_rows(after(parts0[2], mid1))
    relayed = [over_cols(after(across, beside), k) for k in shifts]
    down_own = after(w_down[0], relayed)
    downs = [down_own] + [over_cols(down_own, k) for k in shifts]
    pieces = [mine, across] + [v for pair in zip(beside, relayed) for v in pair]

    def acts(rows):
        return (like((rows, half), BF16), like((rows, half), F32), like((rows, half), F32))

    def tall(part):
        return part.shape[0] // 2

    whole = like((width, half), BF16)
    *first, gate_w, up_w = call(
        functools.partial(forward_first_kernel, cols=cols), 1, 1 + dp,
        acts(tall(parts0[0])) + (whole, whole),
    )(me, parts0[0], *pieces)
    down_w = call(
        functools.partial(down_kernel, cols=cols), 1, cols, like((half, width), BF16)
    )(me, *downs)

    def forward(part):
        return call(forward_kernel, 0, 3, acts(tall(part)))(part, gate_w, up_w)

    def backward(values, parts, kind, *done):
        rows = sum(tall(part) for part in parts)
        return call(
            backward_kernel, 0, 3 + 4 * len(parts), like((rows, width + LANES), kind)
        )(after(gate_w, *done), up_w, down_w, *[v for each in zip(*values) for v in each], *parts)

    def merge(own, came, n):
        return call(merge_kernel, 0, 2, (like((capacity, width + LANES), BF16),) * n)(own, came)

    near0, mid0, last0 = parts0
    acts0 = [first, forward(mid0), forward(last0)]
    acts1 = [forward(near1), forward(mid1)]
    ready = [values[0] for values in acts0 + acts1]
    back_mid1 = backward([acts1[1]], [mid1], BF16, *ready)
    came_mid = over_rows(after(back_mid1, last1))
    acts1.append(forward(after(last1, back_mid1)))
    back_rest1 = backward([acts1[2], acts1[0]], [last1, near1], BF16)
    came_rest = over_rows(after(back_rest1, came_mid))
    kept, sent = call(
        functools.partial(weight_kernel, cols=cols, n_hidden=6), 1, 12,
        (like((down_rows, width), F32), like((cols - 1, down_rows, width), BF16)),
        [pltpu.VMEM((half, width), F32)],
    )(me, after(acts0[0][0], back_rest1), acts0[1][0], acts0[2][0], *[a[0] for a in acts1],
      near0, mid0, last0, near1, mid1, last1)
    back_mid0 = backward([acts0[1]], [mid0], F32, kept)
    mid_blocks = merge(back_mid0, came_mid, middle - here)
    home = {k: flipped(block, k) for k, block in zip(range(here, middle), mid_blocks)}
    grad_came = [over_cols(sent[k - 1], k) for k in shifts]
    back_rest0 = backward(
        [acts0[2], acts0[0]], [last0, near0], F32, kept, *[home[k] for k in range(here, middle)]
    )
    order = [*range(middle, experts), *range(here)]
    rest_blocks = dict(zip(order, merge(back_rest0, came_rest, len(order))))
    home[0] = rest_blocks[0]
    for k in [k for k in order if k > 1]:
        home[k] = flipped(rest_blocks[k], k)
    home[1] = flipped(after(rest_blocks[1], home[2]), 1)
    d_tokens, d_gate = call(
        return_kernel, 0, 2 + experts, (like((per_dev, width), BF16), like((1, per_dev), F32))
    )(dest, prob_row, *[home[k] for k in range(experts)])
    grad_rows = kept
    for value in grad_came:
        grad_rows = grad_rows + value.astype(F32)
    return (d_tokens, d_gate.reshape(per_dev), grad_rows[None])


def solution(mesh):
    placed = (
        P(("dp", "expert"), None),
        P(("dp", "expert"), None),
        P(("dp", "expert")),
        P(("dp", "expert"), None),
        P("expert", "dp", None),
        P("expert", "dp", None),
        P("expert", "dp", None),
    )
    return jax.shard_map(
        body,
        mesh=mesh,
        in_specs=placed,
        out_specs=(P(("dp", "expert"), None), P(("dp", "expert")), P("expert", "dp", None)),
        check_vma=False,
    )
```

```python
import functools

import jax
import jax.numpy as jnp
from jax import lax
from jax.experimental import pallas as pl
from jax.experimental.pallas import tpu as pltpu
from jax.sharding import PartitionSpec as P

F32 = jnp.float32
BF16 = jnp.bfloat16
LANES = 128
PARAMS = pltpu.CompilerParams(vmem_limit_bytes=40 << 20)
VMEM = pl.BlockSpec(memory_space=pltpu.VMEM)
SMEM = pl.BlockSpec(memory_space=pltpu.SMEM)


def like(shape, dtype):
    return jax.ShapeDtypeStruct(shape, dtype)


def call(kernel, n_scalar, n_in, outs, scratch=(), spec=VMEM):
    return pl.pallas_call(
        kernel,
        out_shape=outs,
        in_specs=[SMEM] * n_scalar + [spec] * n_in,
        out_specs=jax.tree.map(lambda _: VMEM, outs),
        scratch_shapes=list(scratch),
        compiler_params=PARAMS,
    )


def dot(left, right, dims):
    return lax.dot_general(left, right, ((dims[:1], dims[1:]), ((), ())), preferred_element_type=F32)


def eye(size):
    rows = lax.broadcasted_iota(jnp.int32, (size, size), 0)
    return rows == lax.broadcasted_iota(jnp.int32, (size, size), 1)


def to_column(row):
    size = row.shape[1]
    spread = jnp.broadcast_to(row, (size, size))
    return jnp.sum(jnp.where(eye(size), spread, jnp.zeros_like(spread)), axis=1, keepdims=True)


def to_row(column):
    size = column.shape[0]
    spread = jnp.broadcast_to(column, (size, size))
    return jnp.sum(jnp.where(eye(size), spread, jnp.zeros_like(spread)), axis=0, keepdims=True)


def dispatch_kernel(me, ids, prob, tokens, cotangent, dest, *blocks):
    per_dev = tokens.shape[0]
    capacity = blocks[0].shape[0] // 2
    slots = len(blocks) * capacity
    id_row = ids[...] ^ me[0]
    id_col = to_column(id_row)
    earlier = lax.broadcasted_iota(jnp.int32, (per_dev, per_dev), 0) < lax.broadcasted_iota(
        jnp.int32, (per_dev, per_dev), 1
    )
    same = jnp.where((id_col == id_row) & earlier, 1, 0)
    dest_row = id_row * capacity + jnp.sum(same, axis=0, keepdims=True)
    dest[...] = dest_row
    pick = jnp.where(
        lax.broadcasted_iota(jnp.int32, (slots, per_dev), 0) == dest_row, 1.0, 0.0
    ).astype(BF16)
    scaled = (to_column(prob[...]) * cotangent[...].astype(F32)).astype(BF16)
    for k, block in enumerate(blocks):
        rows = pick[k * capacity:(k + 1) * capacity, :]
        block[:capacity, :] = dot(rows, tokens[...], (1, 0)).astype(BF16)
        block[capacity:, :] = dot(rows, scaled, (1, 0)).astype(BF16)


def group_kernel(*refs):
    blocks, out = refs[:-1], refs[-1]
    capacity = blocks[0].shape[0] // 2
    tall = len(blocks) * capacity
    for k, block in enumerate(blocks):
        out[k * capacity:(k + 1) * capacity, :] = block[:capacity, :]
        out[tall + k * capacity:tall + (k + 1) * capacity, :] = block[capacity:, :]


def halves_kernel(me, gate, up, mine, other, held, done, *, cols):
    copies = [
        pltpu.make_async_copy(ref, held.at[k], done.at[k]) for k, ref in enumerate((gate, up))
    ]
    for copy in copies:
        copy.start()
    half = gate.shape[1] // 2
    first = me[0] // cols == 0
    for k, copy in enumerate(copies):
        copy.wait()
        low = held[k, :, :half]
        high = held[k, :, half:]
        mine[:, k * half:(k + 1) * half] = jnp.where(first, low, high)
        other[:, k * half:(k + 1) * half] = jnp.where(first, high, low)


def piece_places(me, cols):
    row, col = me // cols, me % cols
    places = [row * cols + col, (1 - row) * cols + col]
    for k in range(1, cols):
        there = (col + cols - k) % cols
        places += [row * cols + there, (1 - row) * cols + there]
    return places


def forward_math(inputs, gate_w, up_w, hidden, slope, silu):
    gate_pre = dot(inputs, gate_w, (1, 0))
    up_pre = dot(inputs, up_w, (1, 0))
    sigmoid_g = jax.nn.sigmoid(gate_pre)
    silu_g = gate_pre * sigmoid_g
    hidden[...] = (silu_g * up_pre).astype(BF16)
    slope[...] = up_pre * sigmoid_g * (1.0 + gate_pre * (1.0 - sigmoid_g))
    silu[...] = silu_g


def token_rows(parts):
    return jnp.concatenate([p[:p.shape[0] // 2, :] for p in parts], axis=0)


def scaled_rows(parts):
    return jnp.concatenate([p[p.shape[0] // 2:, :] for p in parts], axis=0)


def forward_first_kernel(me, part, *refs, cols):
    pieces, (hidden, slope, silu, gate_w, up_w) = refs[:-5], refs[-5:]
    rows = pieces[0].shape[0]
    half = pieces[0].shape[1] // 2
    for piece, place in zip(pieces, piece_places(me[0], cols)):
        at = pl.ds(pl.multiple_of(place * rows, rows), rows)
        gate_w[at, :] = piece[:, :half]
        up_w[at, :] = piece[:, half:]
    forward_math(token_rows([part]), gate_w[...], up_w[...], hidden, slope, silu)


def forward_kernel(part, gate_w, up_w, hidden, slope, silu):
    forward_math(token_rows([part]), gate_w[...], up_w[...], hidden, slope, silu)


def down_kernel(me, *refs, cols):
    pieces, down_w = refs[:-1], refs[-1]
    rows = pieces[0].shape[0]
    for k, piece in enumerate(pieces):
        there = (me[0] % cols + cols - k) % cols
        down_w[pl.ds(pl.multiple_of(there * rows, rows), rows), :] = piece[...]


def backward_kernel(gate_w, up_w, down_w, *refs):
    n = len(refs) // 4
    hidden, slope, silu = (
        jnp.concatenate([r[...] for r in refs[k * n:(k + 1) * n]], axis=0) for k in range(3)
    )
    parts, back = refs[3 * n:4 * n], refs[-1]
    hidden_back = dot(scaled_rows(parts), down_w[...], (1, 1))
    slot_sums = jnp.sum(hidden.astype(F32) * hidden_back, axis=1, keepdims=True)
    grad_gate = (hidden_back * slope).astype(BF16)
    grad_up = (hidden_back * silu).astype(BF16)
    width = back.shape[1] - LANES
    back[:, :width] = (
        dot(grad_gate, gate_w[...], (1, 1)) + dot(grad_up, up_w[...], (1, 1))
    ).astype(back.dtype)
    back[:, width:] = gate_lanes(slot_sums, back.dtype)


def gate_lanes(column, kind):
    column = jnp.broadcast_to(column, (column.shape[0], LANES))
    lane = lax.broadcasted_iota(jnp.int32, column.shape, 1)
    top = column.astype(kind).astype(F32)
    return jnp.where(lane == 0, top, jnp.where(lane == 1, column - top, 0.0)).astype(kind)


def merge_kernel(own, came, *blocks):
    rows, width = blocks[0].shape[0], blocks[0].shape[1] - LANES
    for k, block in enumerate(blocks):
        total = own[k * rows:(k + 1) * rows, :] + came[k * rows:(k + 1) * rows, :].astype(F32)
        block[:, :width] = total[:, :width].astype(BF16)
        block[:, width:] = gate_lanes(jnp.sum(total[:, width:], axis=1, keepdims=True), BF16)


def weight_kernel(me, *refs, cols, n_hidden):
    hiddens, parts, (kept, sent, term) = refs[:n_hidden], refs[n_hidden:-3], refs[-3:]
    hidden = jnp.concatenate([h[...] for h in hiddens], axis=0)
    term[...] = dot(hidden, scaled_rows(parts), (0, 0))
    rows = kept.shape[0]
    col = me[0] % cols
    kept[...] = term[pl.ds(pl.multiple_of(col * rows, rows), rows), :]
    for k in range(1, cols):
        there = (col + k) % cols
        sent[k - 1] = term[pl.ds(pl.multiple_of(there * rows, rows), rows), :].astype(BF16)


def return_kernel(dest, prob, *refs):
    blocks, (d_tokens, d_gate) = refs[:-2], refs[-2:]
    per_dev, width = d_tokens.shape
    back = jnp.concatenate([block[...] for block in blocks], axis=0)
    pick = jnp.where(
        lax.broadcasted_iota(jnp.int32, (back.shape[0], per_dev), 0) == dest[...], 1.0, 0.0
    ).astype(BF16)
    home = dot(pick, back, (0, 0))
    d_tokens[...] = home[:, :width].astype(BF16)
    d_gate[...] = to_row(jnp.sum(home[:, width:], axis=1, keepdims=True)) / prob[...]


def body(tokens, cotangent, gate_prob, bin_ids, w_gate, w_up, w_down):
    experts = lax.axis_size("expert")
    dp = lax.axis_size("dp")
    cols = dp // 2
    per_dev, width = tokens.shape
    ff = w_gate.shape[2]
    half = ff // 2
    gate_rows = w_gate.shape[1]
    down_rows = w_down.shape[1]
    capacity = 3 * per_dev // experts
    slots = experts * capacity
    here = experts // 2
    me = lax.axis_index("dp").astype(jnp.int32).reshape(1)
    my_expert = lax.axis_index("expert").astype(jnp.int32).reshape(1)

    def after(value, *done):
        return lax.optimization_barrier((value,) + done)[0]

    def over_rows(value):
        return lax.ppermute(value, "dp", [(i, (i + cols) % dp) for i in range(dp)])

    def over_cols(value, k):
        return lax.ppermute(
            value, "dp", [(i, i // cols * cols + (i + k) % cols) for i in range(dp)]
        )

    def flipped(value, k):
        return lax.ppermute(value, "expert", [(i, i ^ k) for i in range(experts)])

    shifts = range(1, cols)
    prob_row = gate_prob.reshape(1, per_dev)
    mine, other = call(
        functools.partial(halves_kernel, cols=cols), 1, 2,
        (like((gate_rows, ff), BF16), like((gate_rows, ff), BF16)),
        [pltpu.VMEM((2, gate_rows, ff), BF16), pltpu.SemaphoreType.DMA((2,))],
        pl.BlockSpec(memory_space=pl.ANY),
    )(me, *[pltpu.with_memory_space_constraint(w[0], pltpu.HBM) for w in (w_gate, w_up)])
    dest, *blocks = call(
        dispatch_kernel, 1, 4,
        (like((1, per_dev), jnp.int32),) + (like((2 * capacity, width), BF16),) * experts,
        spec=pl.BlockSpec(),
    )(after(my_expert, mine), bin_ids.reshape(1, per_dev), prob_row, tokens, cotangent)

    across = over_rows(other)
    beside = [over_cols(mine, k) for k in shifts]
    came = {0: blocks[0]}

    def fetch(k, *done):
        came[k] = flipped(after(blocks[k], *done) if done else blocks[k], k)

    fetch(here)
    for k in range(2, here):
        fetch(k, *([came[k - 2]] if k >= 4 else []))
    fetch(here + 1, came[2])
    fetch(1, came[2], came[here])
    for k in range(here + 2, experts):
        fetch(k, came[k - 2])

    def group(flips):
        return call(group_kernel, 0, len(flips), like((2 * capacity * len(flips), width), BF16))(
            *[came[k] for k in flips]
        )

    middle = here + here // 2
    spans = (range(here), range(here, middle), range(middle, experts))
    parts0 = [group(span) for span in spans]
    near1 = over_rows(after(parts0[0], across))
    mid1 = over_rows(after(parts0[1], near1, came[experts - 2]))
    last1 = over_rows(after(parts0[2], mid1))
    relayed = [over_cols(after(across, beside), k) for k in shifts]
    down_own = after(w_down[0], relayed)
    downs = [down_own] + [over_cols(down_own, k) for k in shifts]
    pieces = [mine, across] + [v for pair in zip(beside, relayed) for v in pair]

    def acts(rows):
        return (like((rows, half), BF16), like((rows, half), F32), like((rows, half), F32))

    def tall(part):
        return part.shape[0] // 2

    whole = like((width, half), BF16)
    *first, gate_w, up_w = call(
        functools.partial(forward_first_kernel, cols=cols), 1, 1 + dp,
        acts(tall(parts0[0])) + (whole, whole),
    )(me, parts0[0], *pieces)
    down_w = call(
        functools.partial(down_kernel, cols=cols), 1, cols, like((half, width), BF16)
    )(me, *downs)

    def forward(part):
        return call(forward_kernel, 0, 3, acts(tall(part)))(part, gate_w, up_w)

    def backward(values, parts, kind, *done):
        rows = sum(tall(part) for part in parts)
        return call(
            backward_kernel, 0, 3 + 4 * len(parts), like((rows, width + LANES), kind)
        )(after(gate_w, *done), up_w, down_w, *[v for each in zip(*values) for v in each], *parts)

    def merge(own, came, n):
        return call(merge_kernel, 0, 2, (like((capacity, width + LANES), BF16),) * n)(own, came)

    near0, mid0, last0 = parts0
    acts0 = [first, forward(mid0), forward(last0)]
    acts1 = [forward(near1), forward(mid1)]
    ready = [values[0] for values in acts0 + acts1]
    back_mid1 = backward([acts1[1]], [mid1], BF16, *ready)
    back_mid0 = backward([acts0[1]], [mid0], F32, back_mid1)
    last1 = after(last1, back_mid0)
    came_mid = over_rows(after(back_mid1, last1))
    acts1.append(forward(last1))
    back_rest1 = backward([acts1[2], acts1[0]], [last1, near1], BF16)
    kept, sent = call(
        functools.partial(weight_kernel, cols=cols, n_hidden=6), 1, 12,
        (like((down_rows, width), F32), like((cols - 1, down_rows, width), BF16)),
        [pltpu.VMEM((half, width), F32)],
    )(me, after(acts0[0][0], back_rest1), acts0[1][0], acts0[2][0], *[a[0] for a in acts1],
      near0, mid0, last0, near1, mid1, last1)
    came_rest = over_rows(after(back_rest1, came_mid, kept))
    mid_blocks = merge(after(back_mid0, kept), came_mid, middle - here)
    home = {k: flipped(block, k) for k, block in zip(range(here, middle), mid_blocks)}
    grad_came = [over_cols(sent[k - 1], k) for k in shifts]
    back_rest0 = backward(
        [acts0[2], acts0[0]], [last0, near0], F32, home[here]
    )
    order = [*range(middle, experts), *range(here)]
    rest_blocks = dict(zip(order, merge(after(back_rest0, *[home[k] for k in range(here, middle)]), came_rest, len(order))))
    home[0] = rest_blocks[0]
    for k in [k for k in order if k > 1]:
        home[k] = flipped(rest_blocks[k], k)
    home[1] = flipped(after(rest_blocks[1], home[2]), 1)
    d_tokens, d_gate = call(
        return_kernel, 0, 2 + experts, (like((per_dev, width), BF16), like((1, per_dev), F32))
    )(dest, prob_row, *[home[k] for k in range(experts)])
    grad_rows = kept
    for value in grad_came:
        grad_rows = grad_rows + value.astype(F32)
    return (d_tokens, d_gate.reshape(per_dev), grad_rows[None])


def solution(mesh):
    placed = (
        P(("dp", "expert"), None),
        P(("dp", "expert"), None),
        P(("dp", "expert")),
        P(("dp", "expert"), None),
        P("expert", "dp", None),
        P("expert", "dp", None),
        P("expert", "dp", None),
    )
    return jax.shard_map(
        body,
        mesh=mesh,
        in_specs=placed,
        out_specs=(P(("dp", "expert"), None), P(("dp", "expert")), P("expert", "dp", None)),
        check_vma=False,
    )
```

```python
import functools

import jax
import jax.numpy as jnp
from jax import lax
from jax.experimental import pallas as pl
from jax.experimental.pallas import tpu as pltpu
from jax.sharding import PartitionSpec as P

F32 = jnp.float32
BF16 = jnp.bfloat16
LANES = 128
PARAMS = pltpu.CompilerParams(vmem_limit_bytes=40 << 20)
VMEM = pl.BlockSpec(memory_space=pltpu.VMEM)
SMEM = pl.BlockSpec(memory_space=pltpu.SMEM)


def like(shape, dtype):
    return jax.ShapeDtypeStruct(shape, dtype)


def call(kernel, n_scalar, n_in, outs, scratch=(), spec=VMEM):
    return pl.pallas_call(
        kernel,
        out_shape=outs,
        in_specs=[SMEM] * n_scalar + [spec] * n_in,
        out_specs=jax.tree.map(lambda _: VMEM, outs),
        scratch_shapes=list(scratch),
        compiler_params=PARAMS,
    )


def dot(left, right, dims):
    return lax.dot_general(left, right, ((dims[:1], dims[1:]), ((), ())), preferred_element_type=F32)


def eye(size):
    rows = lax.broadcasted_iota(jnp.int32, (size, size), 0)
    return rows == lax.broadcasted_iota(jnp.int32, (size, size), 1)


def to_column(row):
    size = row.shape[1]
    spread = jnp.broadcast_to(row, (size, size))
    return jnp.sum(jnp.where(eye(size), spread, jnp.zeros_like(spread)), axis=1, keepdims=True)


def to_row(column):
    size = column.shape[0]
    spread = jnp.broadcast_to(column, (size, size))
    return jnp.sum(jnp.where(eye(size), spread, jnp.zeros_like(spread)), axis=0, keepdims=True)


def dispatch_kernel(me, ids, prob, tokens, cotangent, dest, *blocks):
    per_dev = tokens.shape[0]
    capacity = blocks[0].shape[0] // 2
    slots = len(blocks) * capacity
    id_row = ids[...] ^ me[0]
    id_col = to_column(id_row)
    earlier = lax.broadcasted_iota(jnp.int32, (per_dev, per_dev), 0) < lax.broadcasted_iota(
        jnp.int32, (per_dev, per_dev), 1
    )
    same = jnp.where((id_col == id_row) & earlier, 1, 0)
    dest_row = id_row * capacity + jnp.sum(same, axis=0, keepdims=True)
    dest[...] = dest_row
    pick = jnp.where(
        lax.broadcasted_iota(jnp.int32, (slots, per_dev), 0) == dest_row, 1.0, 0.0
    ).astype(BF16)
    scaled = (to_column(prob[...]) * cotangent[...].astype(F32)).astype(BF16)
    for k, block in enumerate(blocks):
        rows = pick[k * capacity:(k + 1) * capacity, :]
        block[:capacity, :] = dot(rows, tokens[...], (1, 0)).astype(BF16)
        block[capacity:, :] = dot(rows, scaled, (1, 0)).astype(BF16)


def group_kernel(*refs):
    blocks, out = refs[:-1], refs[-1]
    capacity = blocks[0].shape[0] // 2
    tall = len(blocks) * capacity
    for k, block in enumerate(blocks):
        out[k * capacity:(k + 1) * capacity, :] = block[:capacity, :]
        out[tall + k * capacity:tall + (k + 1) * capacity, :] = block[capacity:, :]


def halves_kernel(me, gate, up, mine, other, held, done, *, cols):
    copies = [
        pltpu.make_async_copy(ref, held.at[k], done.at[k]) for k, ref in enumerate((gate, up))
    ]
    for copy in copies:
        copy.start()
    half = gate.shape[1] // 2
    first = me[0] // cols == 0
    for k, copy in enumerate(copies):
        copy.wait()
        low = held[k, :, :half]
        high = held[k, :, half:]
        mine[:, k * half:(k + 1) * half] = jnp.where(first, low, high)
        other[:, k * half:(k + 1) * half] = jnp.where(first, high, low)


def piece_places(me, cols):
    row, col = me // cols, me % cols
    places = [row * cols + col, (1 - row) * cols + col]
    for k in range(1, cols):
        there = (col + cols - k) % cols
        places += [row * cols + there, (1 - row) * cols + there]
    return places


def forward_math(inputs, gate_w, up_w, hidden, slope, silu):
    gate_pre = dot(inputs, gate_w, (1, 0))
    up_pre = dot(inputs, up_w, (1, 0))
    sigmoid_g = jax.nn.sigmoid(gate_pre)
    silu_g = gate_pre * sigmoid_g
    hidden[...] = (silu_g * up_pre).astype(BF16)
    slope[...] = up_pre * sigmoid_g * (1.0 + gate_pre * (1.0 - sigmoid_g))
    silu[...] = silu_g


def token_rows(parts):
    return jnp.concatenate([p[:p.shape[0] // 2, :] for p in parts], axis=0)


def scaled_rows(parts):
    return jnp.concatenate([p[p.shape[0] // 2:, :] for p in parts], axis=0)


def forward_first_kernel(me, part, *refs, cols):
    pieces, (hidden, slope, silu, gate_w, up_w) = refs[:-5], refs[-5:]
    rows = pieces[0].shape[0]
    half = pieces[0].shape[1] // 2
    for piece, place in zip(pieces, piece_places(me[0], cols)):
        at = pl.ds(pl.multiple_of(place * rows, rows), rows)
        gate_w[at, :] = piece[:, :half]
        up_w[at, :] = piece[:, half:]
    forward_math(token_rows([part]), gate_w[...], up_w[...], hidden, slope, silu)


def forward_kernel(part, gate_w, up_w, hidden, slope, silu):
    forward_math(token_rows([part]), gate_w[...], up_w[...], hidden, slope, silu)


def down_kernel(me, *refs, cols):
    pieces, down_w = refs[:-1], refs[-1]
    rows = pieces[0].shape[0]
    for k, piece in enumerate(pieces):
        there = (me[0] % cols + cols - k) % cols
        down_w[pl.ds(pl.multiple_of(there * rows, rows), rows), :] = piece[...]


def backward_kernel(gate_w, up_w, down_w, *refs):
    n = len(refs) // 4
    hidden, slope, silu = (
        jnp.concatenate([r[...] for r in refs[k * n:(k + 1) * n]], axis=0) for k in range(3)
    )
    parts, back = refs[3 * n:4 * n], refs[-1]
    hidden_back = dot(scaled_rows(parts), down_w[...], (1, 1))
    slot_sums = jnp.sum(hidden.astype(F32) * hidden_back, axis=1, keepdims=True)
    grad_gate = (hidden_back * slope).astype(BF16)
    grad_up = (hidden_back * silu).astype(BF16)
    width = back.shape[1] - LANES
    back[:, :width] = (
        dot(grad_gate, gate_w[...], (1, 1)) + dot(grad_up, up_w[...], (1, 1))
    ).astype(back.dtype)
    back[:, width:] = gate_lanes(slot_sums, back.dtype)


def gate_lanes(column, kind):
    column = jnp.broadcast_to(column, (column.shape[0], LANES))
    lane = lax.broadcasted_iota(jnp.int32, column.shape, 1)
    top = column.astype(kind).astype(F32)
    return jnp.where(lane == 0, top, jnp.where(lane == 1, column - top, 0.0)).astype(kind)


def merge_kernel(own, came, *blocks):
    rows, width = blocks[0].shape[0], blocks[0].shape[1] - LANES
    for k, block in enumerate(blocks):
        total = own[k * rows:(k + 1) * rows, :] + came[k * rows:(k + 1) * rows, :].astype(F32)
        block[:, :width] = total[:, :width].astype(BF16)
        block[:, width:] = gate_lanes(jnp.sum(total[:, width:], axis=1, keepdims=True), BF16)


def weight_kernel(me, *refs, cols, n_hidden):
    hiddens, parts, (kept, sent, term) = refs[:n_hidden], refs[n_hidden:-3], refs[-3:]
    hidden = jnp.concatenate([h[...] for h in hiddens], axis=0)
    term[...] = dot(hidden, scaled_rows(parts), (0, 0))
    rows = kept.shape[0]
    col = me[0] % cols
    kept[...] = term[pl.ds(pl.multiple_of(col * rows, rows), rows), :]
    for k in range(1, cols):
        there = (col + k) % cols
        sent[k - 1] = term[pl.ds(pl.multiple_of(there * rows, rows), rows), :].astype(BF16)


def return_kernel(dest, prob, *refs):
    blocks, (d_tokens, d_gate) = refs[:-2], refs[-2:]
    per_dev, width = d_tokens.shape
    back = jnp.concatenate([block[...] for block in blocks], axis=0)
    pick = jnp.where(
        lax.broadcasted_iota(jnp.int32, (back.shape[0], per_dev), 0) == dest[...], 1.0, 0.0
    ).astype(BF16)
    home = dot(pick, back, (0, 0))
    d_tokens[...] = home[:, :width].astype(BF16)
    d_gate[...] = to_row(jnp.sum(home[:, width:], axis=1, keepdims=True)) / prob[...]


def body(tokens, cotangent, gate_prob, bin_ids, w_gate, w_up, w_down):
    experts = lax.axis_size("expert")
    dp = lax.axis_size("dp")
    cols = dp // 2
    per_dev, width = tokens.shape
    ff = w_gate.shape[2]
    half = ff // 2
    gate_rows = w_gate.shape[1]
    down_rows = w_down.shape[1]
    capacity = 3 * per_dev // experts
    slots = experts * capacity
    here = experts // 2
    me = lax.axis_index("dp").astype(jnp.int32).reshape(1)
    my_expert = lax.axis_index("expert").astype(jnp.int32).reshape(1)

    def after(value, *done):
        return lax.optimization_barrier((value,) + done)[0]

    def over_rows(value):
        return lax.ppermute(value, "dp", [(i, (i + cols) % dp) for i in range(dp)])

    def over_cols(value, k):
        return lax.ppermute(
            value, "dp", [(i, i // cols * cols + (i + k) % cols) for i in range(dp)]
        )

    def flipped(value, k):
        return lax.ppermute(value, "expert", [(i, i ^ k) for i in range(experts)])

    shifts = range(1, cols)
    prob_row = gate_prob.reshape(1, per_dev)
    mine, other = call(
        functools.partial(halves_kernel, cols=cols), 1, 2,
        (like((gate_rows, ff), BF16), like((gate_rows, ff), BF16)),
        [pltpu.VMEM((2, gate_rows, ff), BF16), pltpu.SemaphoreType.DMA((2,))],
        pl.BlockSpec(memory_space=pl.ANY),
    )(me, *[pltpu.with_memory_space_constraint(w[0], pltpu.HBM) for w in (w_gate, w_up)])
    dest, *blocks = call(
        dispatch_kernel, 1, 4,
        (like((1, per_dev), jnp.int32),) + (like((2 * capacity, width), BF16),) * experts,
        spec=pl.BlockSpec(),
    )(after(my_expert, mine), bin_ids.reshape(1, per_dev), prob_row, tokens, cotangent)

    across = over_rows(other)
    beside = [over_cols(mine, k) for k in shifts]
    came = {0: blocks[0]}

    def fetch(k, *done):
        came[k] = flipped(after(blocks[k], *done) if done else blocks[k], k)

    fetch(here)
    for k in range(2, here):
        fetch(k, *([came[k - 2]] if k >= 4 else []))
    fetch(here + 1, came[2])
    fetch(1, came[2], came[here])
    for k in range(here + 2, experts):
        fetch(k, came[k - 2])

    def group(flips):
        return call(group_kernel, 0, len(flips), like((2 * capacity * len(flips), width), BF16))(
            *[came[k] for k in flips]
        )

    middle = here + 3 * (here // 4)
    spans = (range(here), range(here, middle), range(middle, experts))
    parts0 = [group(span) for span in spans[:2]]
    near1 = over_rows(after(parts0[0], across))
    mid1 = over_rows(after(parts0[1], near1, came[experts - 2]))
    relayed = [over_cols(after(across, beside), k) for k in shifts]
    down_own = after(w_down[0], relayed)
    downs = [down_own] + [over_cols(down_own, k) for k in shifts]
    pieces = [mine, across] + [v for pair in zip(beside, relayed) for v in pair]

    def acts(rows):
        return (like((rows, half), BF16), like((rows, half), F32), like((rows, half), F32))

    def tall(part):
        return part.shape[0] // 2

    whole = like((width, half), BF16)
    *first, gate_w, up_w = call(
        functools.partial(forward_first_kernel, cols=cols), 1, 1 + dp,
        acts(tall(parts0[0])) + (whole, whole),
    )(me, parts0[0], *pieces)
    down_w = call(
        functools.partial(down_kernel, cols=cols), 1, cols, like((half, width), BF16)
    )(me, *downs)

    def forward(part):
        return call(forward_kernel, 0, 3, acts(tall(part)))(part, gate_w, up_w)

    def backward(values, parts, kind, *done):
        rows = sum(tall(part) for part in parts)
        return call(
            backward_kernel, 0, 3 + 4 * len(parts), like((rows, width + LANES), kind)
        )(after(gate_w, *done), up_w, down_w, *[v for each in zip(*values) for v in each], *parts)

    def merge(own, came, n):
        return call(merge_kernel, 0, 2, (like((capacity, width + LANES), BF16),) * n)(own, came)

    near0, mid0 = parts0
    acts0 = [first, forward(mid0)]
    acts1 = [forward(near1)]
    early = [values[0] for values in acts0 + acts1]
    came[experts - 1] = after(came[experts - 1], *early)
    last0 = group(spans[2])
    last1 = over_rows(after(last0, mid1))
    parts0.append(last0)
    acts0.append(forward(last0))
    acts1.append(forward(mid1))
    ready = [values[0] for values in acts0 + acts1]
    back_mid1 = backward([acts1[1]], [mid1], BF16, *ready)
    back_mid0 = backward([acts0[1]], [mid0], F32, back_mid1)
    last1 = after(last1, back_mid0)
    came_mid = over_rows(after(back_mid1, last1))
    acts1.append(forward(last1))
    back_rest1 = backward([acts1[2], acts1[0]], [last1, near1], BF16)
    kept, sent = call(
        functools.partial(weight_kernel, cols=cols, n_hidden=6), 1, 12,
        (like((down_rows, width), F32), like((cols - 1, down_rows, width), BF16)),
        [pltpu.VMEM((half, width), F32)],
    )(me, after(acts0[0][0], back_rest1), acts0[1][0], acts0[2][0], *[a[0] for a in acts1],
      near0, mid0, last0, near1, mid1, last1)
    came_rest = over_rows(after(back_rest1, came_mid, kept))
    mid_blocks = merge(after(back_mid0, kept), came_mid, middle - here)
    home = {k: flipped(block, k) for k, block in zip(range(here, middle), mid_blocks)}
    grad_came = [over_cols(sent[k - 1], k) for k in shifts]
    back_rest0 = backward(
        [acts0[2], acts0[0]], [last0, near0], F32, home[here]
    )
    order = [*range(middle, experts), *range(here)]
    rest_blocks = dict(zip(order, merge(after(back_rest0, home[here], home[here + 1]), came_rest, len(order))))
    home[0] = rest_blocks[0]
    for k in [k for k in order if k > 1]:
        home[k] = flipped(rest_blocks[k], k)
    home[1] = flipped(after(rest_blocks[1], home[2]), 1)
    d_tokens, d_gate = call(
        return_kernel, 0, 2 + experts, (like((per_dev, width), BF16), like((1, per_dev), F32))
    )(dest, prob_row, *[home[k] for k in range(experts)])
    grad_rows = kept
    for value in grad_came:
        grad_rows = grad_rows + value.astype(F32)
    return (d_tokens, d_gate.reshape(per_dev), grad_rows[None])


def solution(mesh):
    placed = (
        P(("dp", "expert"), None),
        P(("dp", "expert"), None),
        P(("dp", "expert")),
        P(("dp", "expert"), None),
        P("expert", "dp", None),
        P("expert", "dp", None),
        P("expert", "dp", None),
    )
    return jax.shard_map(
        body,
        mesh=mesh,
        in_specs=placed,
        out_specs=(P(("dp", "expert"), None), P(("dp", "expert")), P("expert", "dp", None)),
        check_vma=False,
    )
```

```python
import functools

import jax
import jax.numpy as jnp
from jax import lax
from jax.experimental import pallas as pl
from jax.experimental.pallas import tpu as pltpu
from jax.sharding import PartitionSpec as P

F32 = jnp.float32
BF16 = jnp.bfloat16
LANES = 128
GATE_ROWS = 8
PARAMS = pltpu.CompilerParams(vmem_limit_bytes=40 << 20)
VMEM = pl.BlockSpec(memory_space=pltpu.VMEM)
SMEM = pl.BlockSpec(memory_space=pltpu.SMEM)


def like(shape, dtype):
    return jax.ShapeDtypeStruct(shape, dtype)


def call(kernel, n_scalar, n_in, outs, scratch=(), spec=VMEM):
    return pl.pallas_call(
        kernel,
        out_shape=outs,
        in_specs=[SMEM] * n_scalar + [spec] * n_in,
        out_specs=jax.tree.map(lambda _: VMEM, outs),
        scratch_shapes=list(scratch),
        compiler_params=PARAMS,
    )


def dot(left, right, dims):
    return lax.dot_general(left, right, ((dims[:1], dims[1:]), ((), ())), preferred_element_type=F32)


def eye(size):
    rows = lax.broadcasted_iota(jnp.int32, (size, size), 0)
    return rows == lax.broadcasted_iota(jnp.int32, (size, size), 1)


def to_column(row):
    size = row.shape[1]
    spread = jnp.broadcast_to(row, (size, size))
    return jnp.sum(jnp.where(eye(size), spread, jnp.zeros_like(spread)), axis=1, keepdims=True)


def to_row(column):
    size = column.shape[0]
    spread = jnp.broadcast_to(column, (size, size))
    return jnp.sum(jnp.where(eye(size), spread, jnp.zeros_like(spread)), axis=0, keepdims=True)


def dispatch_kernel(me, ids, prob, tokens, cotangent, dest, *blocks):
    per_dev = tokens.shape[0]
    capacity = blocks[0].shape[0] // 2
    slots = len(blocks) * capacity
    id_row = ids[...] ^ me[0]
    id_col = to_column(id_row)
    earlier = lax.broadcasted_iota(jnp.int32, (per_dev, per_dev), 0) < lax.broadcasted_iota(
        jnp.int32, (per_dev, per_dev), 1
    )
    same = jnp.where((id_col == id_row) & earlier, 1, 0)
    dest_row = id_row * capacity + jnp.sum(same, axis=0, keepdims=True)
    dest[...] = dest_row
    pick = jnp.where(
        lax.broadcasted_iota(jnp.int32, (slots, per_dev), 0) == dest_row, 1.0, 0.0
    ).astype(BF16)
    scaled = (to_column(prob[...]) * cotangent[...].astype(F32)).astype(BF16)
    for k, block in enumerate(blocks):
        rows = pick[k * capacity:(k + 1) * capacity, :]
        block[:capacity, :] = dot(rows, tokens[...], (1, 0)).astype(BF16)
        block[capacity:, :] = dot(rows, scaled, (1, 0)).astype(BF16)


def group_kernel(*refs):
    blocks, out = refs[:-1], refs[-1]
    capacity = blocks[0].shape[0] // 2
    tall = len(blocks) * capacity
    for k, block in enumerate(blocks):
        out[k * capacity:(k + 1) * capacity, :] = block[:capacity, :]
        out[tall + k * capacity:tall + (k + 1) * capacity, :] = block[capacity:, :]


def halves_kernel(me, gate, up, mine, other, held, done, *, cols):
    copies = [
        pltpu.make_async_copy(ref, held.at[k], done.at[k]) for k, ref in enumerate((gate, up))
    ]
    for copy in copies:
        copy.start()
    half = gate.shape[1] // 2
    first = me[0] // cols == 0
    for k, copy in enumerate(copies):
        copy.wait()
        low = held[k, :, :half]
        high = held[k, :, half:]
        mine[:, k * half:(k + 1) * half] = jnp.where(first, low, high)
        other[:, k * half:(k + 1) * half] = jnp.where(first, high, low)


def piece_places(me, cols):
    row, col = me // cols, me % cols
    places = [row * cols + col, (1 - row) * cols + col]
    for k in range(1, cols):
        there = (col + cols - k) % cols
        places += [row * cols + there, (1 - row) * cols + there]
    return places


def forward_math(inputs, gate_w, up_w, hidden, slope, silu):
    gate_pre = dot(inputs, gate_w, (1, 0))
    up_pre = dot(inputs, up_w, (1, 0))
    sigmoid_g = jax.nn.sigmoid(gate_pre)
    silu_g = gate_pre * sigmoid_g
    hidden[...] = (silu_g * up_pre).astype(BF16)
    slope[...] = up_pre * sigmoid_g * (1.0 + gate_pre * (1.0 - sigmoid_g))
    silu[...] = silu_g


def token_rows(parts):
    return jnp.concatenate([p[:p.shape[0] // 2, :] for p in parts], axis=0)


def scaled_rows(parts):
    return jnp.concatenate([p[p.shape[0] // 2:, :] for p in parts], axis=0)


def forward_first_kernel(me, part, *refs, cols):
    pieces, (hidden, slope, silu, gate_w, up_w) = refs[:-5], refs[-5:]
    rows = pieces[0].shape[0]
    half = pieces[0].shape[1] // 2
    for piece, place in zip(pieces, piece_places(me[0], cols)):
        at = pl.ds(pl.multiple_of(place * rows, rows), rows)
        gate_w[at, :] = piece[:, :half]
        up_w[at, :] = piece[:, half:]
    forward_math(token_rows([part]), gate_w[...], up_w[...], hidden, slope, silu)


def forward_kernel(part, gate_w, up_w, hidden, slope, silu):
    forward_math(token_rows([part]), gate_w[...], up_w[...], hidden, slope, silu)


def down_kernel(me, *refs, cols):
    pieces, down_w = refs[:-1], refs[-1]
    rows = pieces[0].shape[0]
    for k, piece in enumerate(pieces):
        there = (me[0] % cols + cols - k) % cols
        down_w[pl.ds(pl.multiple_of(there * rows, rows), rows), :] = piece[...]


def backward_kernel(gate_w, up_w, down_w, *refs):
    n = len(refs) // 4
    hidden, slope, silu = (
        jnp.concatenate([r[...] for r in refs[k * n:(k + 1) * n]], axis=0) for k in range(3)
    )
    parts, back = refs[3 * n:4 * n], refs[-1]
    hidden_back = dot(scaled_rows(parts), down_w[...], (1, 1))
    slot_sums = jnp.sum(hidden.astype(F32) * hidden_back, axis=1, keepdims=True)
    grad_gate = (hidden_back * slope).astype(BF16)
    grad_up = (hidden_back * silu).astype(BF16)
    rows = hidden_back.shape[0]
    width = gate_w.shape[0]
    back[:rows, :width] = (
        dot(grad_gate, gate_w[...], (1, 1)) + dot(grad_up, up_w[...], (1, 1))
    ).astype(back.dtype)
    if back.dtype == F32:
        back[:, width:] = gate_lanes(slot_sums, F32)
    else:
        line = to_row(slot_sums)
        top = line.astype(BF16).astype(F32)
        place = lax.broadcasted_iota(jnp.int32, (GATE_ROWS, rows), 0)
        back[rows:, :] = jnp.zeros((GATE_ROWS, width), BF16)
        back[rows:, :rows] = jnp.where(
            place == 0, top, jnp.where(place == 1, line - top, 0.0)
        ).astype(BF16)


def gate_lanes(column, kind):
    column = jnp.broadcast_to(column, (column.shape[0], LANES))
    lane = lax.broadcasted_iota(jnp.int32, column.shape, 1)
    top = column.astype(kind).astype(F32)
    return jnp.where(lane == 0, top, jnp.where(lane == 1, column - top, 0.0)).astype(kind)


def merge_kernel(own, came, *blocks):
    rows, width = blocks[0].shape[0], blocks[0].shape[1] - LANES
    tall = own.shape[0]
    came_gates = to_column(jnp.sum(came[tall:, :tall].astype(F32), axis=0, keepdims=True))
    for k, block in enumerate(blocks):
        at = slice(k * rows, (k + 1) * rows)
        block[:, :width] = (own[at, :width] + came[at, :].astype(F32)).astype(BF16)
        gates = jnp.sum(own[at, width:], axis=1, keepdims=True) + came_gates[at, :]
        block[:, width:] = gate_lanes(gates, BF16)


def weight_kernel(me, *refs, cols, n_hidden):
    hiddens, parts, (kept, sent, term) = refs[:n_hidden], refs[n_hidden:-3], refs[-3:]
    hidden = jnp.concatenate([h[...] for h in hiddens], axis=0)
    term[...] = dot(hidden, scaled_rows(parts), (0, 0))
    rows = kept.shape[0]
    col = me[0] % cols
    kept[...] = term[pl.ds(pl.multiple_of(col * rows, rows), rows), :]
    for k in range(1, cols):
        there = (col + k) % cols
        sent[k - 1] = term[pl.ds(pl.multiple_of(there * rows, rows), rows), :].astype(BF16)


def return_kernel(dest, prob, *refs):
    blocks, (d_tokens, d_gate) = refs[:-2], refs[-2:]
    per_dev, width = d_tokens.shape
    back = jnp.concatenate([block[...] for block in blocks], axis=0)
    pick = jnp.where(
        lax.broadcasted_iota(jnp.int32, (back.shape[0], per_dev), 0) == dest[...], 1.0, 0.0
    ).astype(BF16)
    home = dot(pick, back, (0, 0))
    d_tokens[...] = home[:, :width].astype(BF16)
    d_gate[...] = to_row(jnp.sum(home[:, width:], axis=1, keepdims=True)) / prob[...]


def body(tokens, cotangent, gate_prob, bin_ids, w_gate, w_up, w_down):
    experts = lax.axis_size("expert")
    dp = lax.axis_size("dp")
    cols = dp // 2
    per_dev, width = tokens.shape
    ff = w_gate.shape[2]
    half = ff // 2
    gate_rows = w_gate.shape[1]
    down_rows = w_down.shape[1]
    capacity = 3 * per_dev // experts
    slots = experts * capacity
    here = experts // 2
    me = lax.axis_index("dp").astype(jnp.int32).reshape(1)
    my_expert = lax.axis_index("expert").astype(jnp.int32).reshape(1)

    def after(value, *done):
        return lax.optimization_barrier((value,) + done)[0]

    def over_rows(value):
        return lax.ppermute(value, "dp", [(i, (i + cols) % dp) for i in range(dp)])

    def over_cols(value, k):
        return lax.ppermute(
            value, "dp", [(i, i // cols * cols + (i + k) % cols) for i in range(dp)]
        )

    def flipped(value, k):
        return lax.ppermute(value, "expert", [(i, i ^ k) for i in range(experts)])

    shifts = range(1, cols)
    prob_row = gate_prob.reshape(1, per_dev)
    mine, other = call(
        functools.partial(halves_kernel, cols=cols), 1, 2,
        (like((gate_rows, ff), BF16), like((gate_rows, ff), BF16)),
        [pltpu.VMEM((2, gate_rows, ff), BF16), pltpu.SemaphoreType.DMA((2,))],
        pl.BlockSpec(memory_space=pl.ANY),
    )(me, *[pltpu.with_memory_space_constraint(w[0], pltpu.HBM) for w in (w_gate, w_up)])
    dest, *blocks = call(
        dispatch_kernel, 1, 4,
        (like((1, per_dev), jnp.int32),) + (like((2 * capacity, width), BF16),) * experts,
        spec=pl.BlockSpec(),
    )(after(my_expert, mine), bin_ids.reshape(1, per_dev), prob_row, tokens, cotangent)

    across = over_rows(other)
    beside = [over_cols(mine, k) for k in shifts]
    came = {0: blocks[0]}

    def fetch(k, *done):
        came[k] = flipped(after(blocks[k], *done) if done else blocks[k], k)

    fetch(here)
    for k in range(2, here):
        fetch(k, *([came[k - 2]] if k >= 4 else []))
    fetch(here + 1, came[2])
    fetch(1, came[2], came[here])
    for k in range(here + 2, experts):
        fetch(k, came[k - 2])

    def group(flips):
        return call(group_kernel, 0, len(flips), like((2 * capacity * len(flips), width), BF16))(
            *[came[k] for k in flips]
        )

    middle = here + 3 * (here // 4)
    spans = (range(here), range(here, middle), range(middle, experts))
    parts0 = [group(span) for span in spans[:2]]
    near1 = over_rows(after(parts0[0], across))
    mid1 = over_rows(after(parts0[1], near1, came[experts - 2]))
    relayed = [over_cols(after(across, beside), k) for k in shifts]
    down_own = after(w_down[0], relayed)
    downs = [down_own] + [over_cols(down_own, k) for k in shifts]
    pieces = [mine, across] + [v for pair in zip(beside, relayed) for v in pair]

    def acts(rows):
        return (like((rows, half), BF16), like((rows, half), F32), like((rows, half), F32))

    def tall(part):
        return part.shape[0] // 2

    whole = like((width, half), BF16)
    *first, gate_w, up_w = call(
        functools.partial(forward_first_kernel, cols=cols), 1, 1 + dp,
        acts(tall(parts0[0])) + (whole, whole),
    )(me, parts0[0], *pieces)
    down_w = call(
        functools.partial(down_kernel, cols=cols), 1, cols, like((half, width), BF16)
    )(me, *downs)

    def forward(part):
        return call(forward_kernel, 0, 3, acts(tall(part)))(part, gate_w, up_w)

    def backward(values, parts, kind, *done):
        rows = sum(tall(part) for part in parts)
        return call(
            backward_kernel, 0, 3 + 4 * len(parts),
            like((rows, width + LANES) if kind == F32 else (rows + GATE_ROWS, width), kind),
        )(after(gate_w, *done), up_w, down_w, *[v for each in zip(*values) for v in each], *parts)

    def merge(own, came, n):
        return call(merge_kernel, 0, 2, (like((capacity, width + LANES), BF16),) * n)(own, came)

    near0, mid0 = parts0
    acts0 = [first, forward(mid0)]
    acts1 = [forward(near1)]
    early = [values[0] for values in acts0 + acts1]
    came[experts - 1] = after(came[experts - 1], *early)
    last0 = group(spans[2])
    last1 = over_rows(after(last0, near1))
    parts0.append(last0)
    acts0.append(forward(last0))
    acts1.append(forward(mid1))
    ready = [values[0] for values in acts0 + acts1]
    back_mid1 = backward([acts1[1]], [mid1], BF16, *ready)
    back_mid0 = backward([acts0[1]], [mid0], F32, back_mid1)
    last1 = after(last1, back_mid0)
    came_mid = over_rows(after(back_mid1, last1))
    acts1.append(forward(last1))
    back_rest1 = backward([acts1[2], acts1[0]], [last1, near1], BF16)
    kept, sent = call(
        functools.partial(weight_kernel, cols=cols, n_hidden=6), 1, 12,
        (like((down_rows, width), F32), like((cols - 1, down_rows, width), BF16)),
        [pltpu.VMEM((half, width), F32)],
    )(me, after(acts0[0][0], back_rest1), acts0[1][0], acts0[2][0], *[a[0] for a in acts1],
      near0, mid0, last0, near1, mid1, last1)
    came_rest = over_rows(after(back_rest1, came_mid, kept))
    mid_blocks = merge(after(back_mid0, kept), came_mid, middle - here)
    home = {k: flipped(block, k) for k, block in zip(range(here, middle), mid_blocks)}
    grad_came = [over_cols(sent[k - 1], k) for k in shifts]
    back_rest0 = backward(
        [acts0[2], acts0[0]], [last0, near0], F32, home[here]
    )
    order = [*range(middle, experts), *range(here)]
    rest_blocks = dict(zip(order, merge(after(back_rest0, home[here], home[here + 1]), came_rest, len(order))))
    home[0] = rest_blocks[0]
    for k in [k for k in order if k > 1]:
        home[k] = flipped(rest_blocks[k], k)
    home[1] = flipped(after(rest_blocks[1], home[2]), 1)
    d_tokens, d_gate = call(
        return_kernel, 0, 2 + experts, (like((per_dev, width), BF16), like((1, per_dev), F32))
    )(dest, prob_row, *[home[k] for k in range(experts)])
    grad_rows = kept
    for value in grad_came:
        grad_rows = grad_rows + value.astype(F32)
    return (d_tokens, d_gate.reshape(per_dev), grad_rows[None])


def solution(mesh):
    placed = (
        P(("dp", "expert"), None),
        P(("dp", "expert"), None),
        P(("dp", "expert")),
        P(("dp", "expert"), None),
        P("expert", "dp", None),
        P("expert", "dp", None),
        P("expert", "dp", None),
    )
    return jax.shard_map(
        body,
        mesh=mesh,
        in_specs=placed,
        out_specs=(P(("dp", "expert"), None), P(("dp", "expert")), P("expert", "dp", None)),
        check_vma=False,
    )
```

```python
import functools

import jax
import jax.numpy as jnp
from jax import lax
from jax.experimental import pallas as pl
from jax.experimental.pallas import tpu as pltpu
from jax.sharding import PartitionSpec as P

F32 = jnp.float32
BF16 = jnp.bfloat16
LANES = 128
GATE_ROWS = 8
PARAMS = pltpu.CompilerParams(vmem_limit_bytes=40 << 20)
VMEM = pl.BlockSpec(memory_space=pltpu.VMEM)
SMEM = pl.BlockSpec(memory_space=pltpu.SMEM)


def like(shape, dtype):
    return jax.ShapeDtypeStruct(shape, dtype)


def call(kernel, n_scalar, n_in, outs, scratch=(), spec=VMEM):
    return pl.pallas_call(
        kernel,
        out_shape=outs,
        in_specs=[SMEM] * n_scalar + [spec] * n_in,
        out_specs=jax.tree.map(lambda _: VMEM, outs),
        scratch_shapes=list(scratch),
        compiler_params=PARAMS,
    )


def dot(left, right, dims):
    return lax.dot_general(left, right, ((dims[:1], dims[1:]), ((), ())), preferred_element_type=F32)


def eye(size):
    rows = lax.broadcasted_iota(jnp.int32, (size, size), 0)
    return rows == lax.broadcasted_iota(jnp.int32, (size, size), 1)


def to_column(row):
    size = row.shape[1]
    spread = jnp.broadcast_to(row, (size, size))
    return jnp.sum(jnp.where(eye(size), spread, jnp.zeros_like(spread)), axis=1, keepdims=True)


def to_row(column):
    size = column.shape[0]
    spread = jnp.broadcast_to(column, (size, size))
    return jnp.sum(jnp.where(eye(size), spread, jnp.zeros_like(spread)), axis=0, keepdims=True)


def dispatch_kernel(me, ids, prob, tokens, cotangent, dest, *blocks):
    per_dev = tokens.shape[0]
    capacity = blocks[0].shape[0] // 2
    slots = len(blocks) * capacity
    id_row = ids[...] ^ me[0]
    id_col = to_column(id_row)
    earlier = lax.broadcasted_iota(jnp.int32, (per_dev, per_dev), 0) < lax.broadcasted_iota(
        jnp.int32, (per_dev, per_dev), 1
    )
    same = jnp.where((id_col == id_row) & earlier, 1, 0)
    dest_row = id_row * capacity + jnp.sum(same, axis=0, keepdims=True)
    dest[...] = dest_row
    pick = jnp.where(
        lax.broadcasted_iota(jnp.int32, (slots, per_dev), 0) == dest_row, 1.0, 0.0
    ).astype(BF16)
    scaled = (to_column(prob[...]) * cotangent[...].astype(F32)).astype(BF16)
    for k, block in enumerate(blocks):
        rows = pick[k * capacity:(k + 1) * capacity, :]
        block[:capacity, :] = dot(rows, tokens[...], (1, 0)).astype(BF16)
        block[capacity:, :] = dot(rows, scaled, (1, 0)).astype(BF16)


def group_kernel(*refs):
    blocks, out = refs[:-1], refs[-1]
    capacity = blocks[0].shape[0] // 2
    tall = len(blocks) * capacity
    for k, block in enumerate(blocks):
        out[k * capacity:(k + 1) * capacity, :] = block[:capacity, :]
        out[tall + k * capacity:tall + (k + 1) * capacity, :] = block[capacity:, :]


def halves_kernel(me, gate, up, mine, other, held, done, *, cols):
    copies = [
        pltpu.make_async_copy(ref, held.at[k], done.at[k]) for k, ref in enumerate((gate, up))
    ]
    for copy in copies:
        copy.start()
    half = gate.shape[1] // 2
    first = me[0] // cols == 0
    for k, copy in enumerate(copies):
        copy.wait()
        low = held[k, :, :half]
        high = held[k, :, half:]
        mine[:, k * half:(k + 1) * half] = jnp.where(first, low, high)
        other[:, k * half:(k + 1) * half] = jnp.where(first, high, low)


def piece_places(me, cols):
    row, col = me // cols, me % cols
    places = [row * cols + col, (1 - row) * cols + col]
    for k in range(1, cols):
        there = (col + cols - k) % cols
        places += [row * cols + there, (1 - row) * cols + there]
    return places


def forward_math(inputs, gate_w, up_w, hidden, slope, silu):
    gate_pre = dot(inputs, gate_w, (1, 0))
    up_pre = dot(inputs, up_w, (1, 0))
    sigmoid_g = jax.nn.sigmoid(gate_pre)
    silu_g = gate_pre * sigmoid_g
    hidden[...] = (silu_g * up_pre).astype(BF16)
    slope[...] = up_pre * sigmoid_g * (1.0 + gate_pre * (1.0 - sigmoid_g))
    silu[...] = silu_g


def token_rows(parts):
    return jnp.concatenate([p[:p.shape[0] // 2, :] for p in parts], axis=0)


def scaled_rows(parts):
    return jnp.concatenate([p[p.shape[0] // 2:, :] for p in parts], axis=0)


def forward_first_kernel(me, part, *refs, cols):
    pieces, (hidden, slope, silu, gate_w, up_w) = refs[:-5], refs[-5:]
    rows = pieces[0].shape[0]
    half = pieces[0].shape[1] // 2
    for piece, place in zip(pieces, piece_places(me[0], cols)):
        at = pl.ds(pl.multiple_of(place * rows, rows), rows)
        gate_w[at, :] = piece[:, :half]
        up_w[at, :] = piece[:, half:]
    forward_math(token_rows([part]), gate_w[...], up_w[...], hidden, slope, silu)


def forward_kernel(part, gate_w, up_w, hidden, slope, silu):
    forward_math(token_rows([part]), gate_w[...], up_w[...], hidden, slope, silu)


def down_kernel(me, *refs, cols):
    pieces, down_w = refs[:-1], refs[-1]
    rows = pieces[0].shape[0]
    for k, piece in enumerate(pieces):
        there = (me[0] % cols + cols - k) % cols
        down_w[pl.ds(pl.multiple_of(there * rows, rows), rows), :] = piece[...]


def backward_kernel(gate_w, up_w, down_w, *refs):
    n = len(refs) // 4
    hidden, slope, silu = (
        jnp.concatenate([r[...] for r in refs[k * n:(k + 1) * n]], axis=0) for k in range(3)
    )
    parts, back = refs[3 * n:4 * n], refs[-1]
    hidden_back = dot(scaled_rows(parts), down_w[...], (1, 1))
    slot_sums = jnp.sum(hidden.astype(F32) * hidden_back, axis=1, keepdims=True)
    grad_gate = (hidden_back * slope).astype(BF16)
    grad_up = (hidden_back * silu).astype(BF16)
    rows = hidden_back.shape[0]
    width = gate_w.shape[0]
    back[:rows, :width] = (
        dot(grad_gate, gate_w[...], (1, 1)) + dot(grad_up, up_w[...], (1, 1))
    ).astype(back.dtype)
    if back.dtype == F32:
        back[:, width:] = gate_lanes(slot_sums, F32)
    else:
        line = to_row(slot_sums)
        top = line.astype(BF16).astype(F32)
        place = lax.broadcasted_iota(jnp.int32, (GATE_ROWS, rows), 0)
        back[rows:, :] = jnp.zeros((GATE_ROWS, width), BF16)
        back[rows:, :rows] = jnp.where(
            place == 0, top, jnp.where(place == 1, line - top, 0.0)
        ).astype(BF16)


def gate_lanes(column, kind):
    column = jnp.broadcast_to(column, (column.shape[0], LANES))
    lane = lax.broadcasted_iota(jnp.int32, column.shape, 1)
    top = column.astype(kind).astype(F32)
    return jnp.where(lane == 0, top, jnp.where(lane == 1, column - top, 0.0)).astype(kind)


def merge_kernel(own, came, *blocks):
    tall = own.shape[0]
    rows, width = tall // len(blocks), own.shape[1] - LANES
    came_gates = to_column(jnp.sum(came[tall:, :tall].astype(F32), axis=0, keepdims=True))
    strip = blocks[0].shape[0]
    for k, block in enumerate(blocks):
        for j in range(rows // strip):
            at = slice(k * rows + j * strip, k * rows + (j + 1) * strip)
            block[:, j * width:(j + 1) * width] = (own[at, :width] + came[at, :].astype(F32)).astype(BF16)
        at = slice(k * rows, (k + 1) * rows)
        line = to_row(jnp.sum(own[at, width:], axis=1, keepdims=True) + came_gates[at, :])
        top = line.astype(BF16).astype(F32)
        place = lax.broadcasted_iota(jnp.int32, (strip, rows), 0)
        start = rows // strip * width
        block[:, start:] = jnp.zeros((strip, LANES), BF16)
        block[:, start:start + rows] = jnp.where(
            place == 0, top, jnp.where(place == 1, line - top, 0.0)
        ).astype(BF16)


def weight_kernel(me, *refs, cols, n_hidden):
    hiddens, parts, (kept, sent, term) = refs[:n_hidden], refs[n_hidden:-3], refs[-3:]
    hidden = jnp.concatenate([h[...] for h in hiddens], axis=0)
    term[...] = dot(hidden, scaled_rows(parts), (0, 0))
    rows = kept.shape[0]
    col = me[0] % cols
    kept[...] = term[pl.ds(pl.multiple_of(col * rows, rows), rows), :]
    for k in range(1, cols):
        there = (col + k) % cols
        sent[k - 1] = term[pl.ds(pl.multiple_of(there * rows, rows), rows), :].astype(BF16)


def return_kernel(dest, prob, *refs):
    blocks, (d_tokens, d_gate) = refs[:-2], refs[-2:]
    per_dev, width = d_tokens.shape
    strip = blocks[0].shape[0]
    n = (blocks[0].shape[1] - LANES) // width
    rows = n * strip
    dest_col = to_column(dest[...])
    strips, total = [], jnp.zeros((per_dev, 1), F32)
    for k, block in enumerate(blocks):
        strips += [block[:, j * width:(j + 1) * width] for j in range(n)]
        line = jnp.sum(block[:, n * width:n * width + rows].astype(F32), axis=0, keepdims=True)
        here = lax.broadcasted_iota(jnp.int32, (per_dev, rows), 1) + k * rows == dest_col
        total = total + jnp.sum(
            jnp.where(here, jnp.broadcast_to(line, (per_dev, rows)), 0.0), axis=1, keepdims=True
        )
    back = jnp.concatenate(strips, axis=0)
    pick = jnp.where(
        lax.broadcasted_iota(jnp.int32, (back.shape[0], per_dev), 0) == dest[...], 1.0, 0.0
    ).astype(BF16)
    d_tokens[...] = dot(pick, back, (0, 0)).astype(BF16)
    d_gate[...] = to_row(total) / prob[...]


def body(tokens, cotangent, gate_prob, bin_ids, w_gate, w_up, w_down):
    experts = lax.axis_size("expert")
    dp = lax.axis_size("dp")
    cols = dp // 2
    per_dev, width = tokens.shape
    ff = w_gate.shape[2]
    half = ff // 2
    gate_rows = w_gate.shape[1]
    down_rows = w_down.shape[1]
    capacity = 3 * per_dev // experts
    slots = experts * capacity
    strip = 8 if capacity % 8 == 0 else capacity
    here = experts // 2
    me = lax.axis_index("dp").astype(jnp.int32).reshape(1)
    my_expert = lax.axis_index("expert").astype(jnp.int32).reshape(1)

    def after(value, *done):
        return lax.optimization_barrier((value,) + done)[0]

    def over_rows(value):
        return lax.ppermute(value, "dp", [(i, (i + cols) % dp) for i in range(dp)])

    def over_cols(value, k):
        return lax.ppermute(
            value, "dp", [(i, i // cols * cols + (i + k) % cols) for i in range(dp)]
        )

    def flipped(value, k):
        return lax.ppermute(value, "expert", [(i, i ^ k) for i in range(experts)])

    shifts = range(1, cols)
    prob_row = gate_prob.reshape(1, per_dev)
    mine, other = call(
        functools.partial(halves_kernel, cols=cols), 1, 2,
        (like((gate_rows, ff), BF16), like((gate_rows, ff), BF16)),
        [pltpu.VMEM((2, gate_rows, ff), BF16), pltpu.SemaphoreType.DMA((2,))],
        pl.BlockSpec(memory_space=pl.ANY),
    )(me, *[pltpu.with_memory_space_constraint(w[0], pltpu.HBM) for w in (w_gate, w_up)])
    dest, *blocks = call(
        dispatch_kernel, 1, 4,
        (like((1, per_dev), jnp.int32),) + (like((2 * capacity, width), BF16),) * experts,
        spec=pl.BlockSpec(),
    )(after(my_expert, mine), bin_ids.reshape(1, per_dev), prob_row, tokens, cotangent)

    across = over_rows(other)
    beside = [over_cols(mine, k) for k in shifts]
    came = {0: blocks[0]}

    def fetch(k, *done):
        came[k] = flipped(after(blocks[k], *done) if done else blocks[k], k)

    fetch(here)
    for k in range(2, here):
        fetch(k, *([came[k - 2]] if k >= 4 else []))
    fetch(here + 1, came[2])
    fetch(1, came[2], came[here])
    for k in range(here + 2, experts):
        fetch(k, came[k - 2])

    def group(flips):
        return call(group_kernel, 0, len(flips), like((2 * capacity * len(flips), width), BF16))(
            *[came[k] for k in flips]
        )

    middle = here + 3 * (here // 4)
    spans = (range(here), range(here, middle), range(middle, experts))
    parts0 = [group(span) for span in spans[:2]]
    near1 = over_rows(after(parts0[0], across))
    mid1 = over_rows(after(parts0[1], near1, came[experts - 2]))
    relayed = [over_cols(after(across, beside), k) for k in shifts]
    down_own = after(w_down[0], relayed, near1)
    downs = [down_own] + [over_cols(down_own, k) for k in shifts]
    pieces = [mine, across] + [v for pair in zip(beside, relayed) for v in pair]

    def acts(rows):
        return (like((rows, half), BF16), like((rows, half), F32), like((rows, half), F32))

    def tall(part):
        return part.shape[0] // 2

    whole = like((width, half), BF16)
    *first, gate_w, up_w = call(
        functools.partial(forward_first_kernel, cols=cols), 1, 1 + dp,
        acts(tall(parts0[0])) + (whole, whole),
    )(me, parts0[0], *pieces)
    down_w = call(
        functools.partial(down_kernel, cols=cols), 1, cols, like((half, width), BF16)
    )(me, *downs)

    def forward(part):
        return call(forward_kernel, 0, 3, acts(tall(part)))(part, gate_w, up_w)

    def backward(values, parts, kind, *done):
        rows = sum(tall(part) for part in parts)
        return call(
            backward_kernel, 0, 3 + 4 * len(parts),
            like((rows, width + LANES) if kind == F32 else (rows + GATE_ROWS, width), kind),
        )(after(gate_w, *done), up_w, down_w, *[v for each in zip(*values) for v in each], *parts)

    def merge(own, came, n):
        block = like((strip, capacity // strip * width + LANES), BF16)
        return call(merge_kernel, 0, 2, (block,) * n)(own, came)

    near0, mid0 = parts0
    acts0 = [first, forward(mid0)]
    acts1 = [forward(near1)]
    early = [values[0] for values in acts0 + acts1]
    came[experts - 1] = after(came[experts - 1], *early)
    last0 = group(spans[2])
    last1 = over_rows(after(last0, near1))
    parts0.append(last0)
    acts0.append(forward(last0))
    acts1.append(forward(mid1))
    ready = [values[0] for values in acts0 + acts1]
    back_mid1 = backward([acts1[1]], [mid1], BF16, *ready)
    back_mid0 = backward([acts0[1]], [mid0], F32, back_mid1)
    last1 = after(last1, back_mid0)
    came_mid = over_rows(after(back_mid1, last1))
    acts1.append(forward(last1))
    back_rest1 = backward([acts1[2], acts1[0]], [last1, near1], BF16)
    kept, sent = call(
        functools.partial(weight_kernel, cols=cols, n_hidden=6), 1, 12,
        (like((down_rows, width), F32), like((cols - 1, down_rows, width), BF16)),
        [pltpu.VMEM((half, width), F32)],
    )(me, after(acts0[0][0], back_rest1), acts0[1][0], acts0[2][0], *[a[0] for a in acts1],
      near0, mid0, last0, near1, mid1, last1)
    came_rest = over_rows(after(back_rest1, came_mid, kept))
    mid_blocks = merge(after(back_mid0, kept), came_mid, middle - here)
    home = {k: flipped(block, k) for k, block in zip(range(here, middle), mid_blocks)}
    grad_came = [over_cols(sent[k - 1], k) for k in shifts]
    back_rest0 = backward(
        [acts0[2], acts0[0]], [last0, near0], F32, home[here]
    )
    order = [*range(middle, experts), *range(here)]
    rest_blocks = dict(zip(order, merge(after(back_rest0, home[here], home[here + 1]), came_rest, len(order))))
    home[0] = rest_blocks[0]
    for k in [k for k in order if k > 1]:
        home[k] = flipped(rest_blocks[k], k)
    home[1] = flipped(after(rest_blocks[1], home[2]), 1)
    d_tokens, d_gate = call(
        return_kernel, 0, 2 + experts, (like((per_dev, width), BF16), like((1, per_dev), F32))
    )(dest, prob_row, *[home[k] for k in range(experts)])
    grad_rows = kept
    for value in grad_came:
        grad_rows = grad_rows + value.astype(F32)
    return (d_tokens, d_gate.reshape(per_dev), grad_rows[None])


def solution(mesh):
    placed = (
        P(("dp", "expert"), None),
        P(("dp", "expert"), None),
        P(("dp", "expert")),
        P(("dp", "expert"), None),
        P("expert", "dp", None),
        P("expert", "dp", None),
        P("expert", "dp", None),
    )
    return jax.shard_map(
        body,
        mesh=mesh,
        in_specs=placed,
        out_specs=(P(("dp", "expert"), None), P(("dp", "expert")), P("expert", "dp", None)),
        check_vma=False,
    )
```

```python
import functools

import jax
import jax.numpy as jnp
from jax import lax
from jax.experimental import pallas as pl
from jax.experimental.pallas import tpu as pltpu
from jax.sharding import PartitionSpec as P

F32 = jnp.float32
BF16 = jnp.bfloat16
LANES = 128
GATE_ROWS = 8
PARAMS = pltpu.CompilerParams(vmem_limit_bytes=40 << 20)
VMEM = pl.BlockSpec(memory_space=pltpu.VMEM)
SMEM = pl.BlockSpec(memory_space=pltpu.SMEM)


def like(shape, dtype):
    return jax.ShapeDtypeStruct(shape, dtype)


def call(kernel, n_scalar, n_in, outs, scratch=(), spec=VMEM):
    return pl.pallas_call(
        kernel,
        out_shape=outs,
        in_specs=[SMEM] * n_scalar + [spec] * n_in,
        out_specs=jax.tree.map(lambda _: VMEM, outs),
        scratch_shapes=list(scratch),
        compiler_params=PARAMS,
    )


def dot(left, right, dims):
    return lax.dot_general(left, right, ((dims[:1], dims[1:]), ((), ())), preferred_element_type=F32)


def eye(size):
    rows = lax.broadcasted_iota(jnp.int32, (size, size), 0)
    return rows == lax.broadcasted_iota(jnp.int32, (size, size), 1)


def to_column(row):
    size = row.shape[1]
    spread = jnp.broadcast_to(row, (size, size))
    return jnp.sum(jnp.where(eye(size), spread, jnp.zeros_like(spread)), axis=1, keepdims=True)


def to_row(column):
    size = column.shape[0]
    spread = jnp.broadcast_to(column, (size, size))
    return jnp.sum(jnp.where(eye(size), spread, jnp.zeros_like(spread)), axis=0, keepdims=True)


def dispatch_kernel(me, ids, prob, tokens, cotangent, dest, *blocks):
    per_dev = tokens.shape[0]
    capacity = blocks[0].shape[0] // 2
    slots = len(blocks) * capacity
    id_row = ids[...] ^ me[0]
    id_col = to_column(id_row)
    earlier = lax.broadcasted_iota(jnp.int32, (per_dev, per_dev), 0) < lax.broadcasted_iota(
        jnp.int32, (per_dev, per_dev), 1
    )
    same = jnp.where((id_col == id_row) & earlier, 1, 0)
    dest_row = id_row * capacity + jnp.sum(same, axis=0, keepdims=True)
    dest[...] = dest_row
    pick = jnp.where(
        lax.broadcasted_iota(jnp.int32, (slots, per_dev), 0) == dest_row, 1.0, 0.0
    ).astype(BF16)
    scaled = (to_column(prob[...]) * cotangent[...].astype(F32)).astype(BF16)
    for k, block in enumerate(blocks):
        rows = pick[k * capacity:(k + 1) * capacity, :]
        block[:capacity, :] = dot(rows, tokens[...], (1, 0)).astype(BF16)
        block[capacity:, :] = dot(rows, scaled, (1, 0)).astype(BF16)


def group_kernel(*refs):
    blocks, out = refs[:-1], refs[-1]
    capacity = blocks[0].shape[0] // 2
    tall = len(blocks) * capacity
    for k, block in enumerate(blocks):
        out[k * capacity:(k + 1) * capacity, :] = block[:capacity, :]
        out[tall + k * capacity:tall + (k + 1) * capacity, :] = block[capacity:, :]


def halves_kernel(me, gate, up, mine, other, held, done, *, cols):
    copies = [
        pltpu.make_async_copy(ref, held.at[k], done.at[k]) for k, ref in enumerate((gate, up))
    ]
    for copy in copies:
        copy.start()
    half = gate.shape[1] // 2
    first = me[0] // cols == 0
    for k, copy in enumerate(copies):
        copy.wait()
        low = held[k, :, :half]
        high = held[k, :, half:]
        mine[:, k * half:(k + 1) * half] = jnp.where(first, low, high)
        other[:, k * half:(k + 1) * half] = jnp.where(first, high, low)


def piece_places(me, cols):
    row, col = me // cols, me % cols
    places = [row * cols + col, (1 - row) * cols + col]
    for k in range(1, cols):
        there = (col + cols - k) % cols
        places += [row * cols + there, (1 - row) * cols + there]
    return places


def forward_math(inputs, gate_w, up_w, hidden, slope, silu):
    gate_pre = dot(inputs, gate_w, (1, 0))
    up_pre = dot(inputs, up_w, (1, 0))
    sigmoid_g = jax.nn.sigmoid(gate_pre)
    silu_g = gate_pre * sigmoid_g
    hidden[...] = (silu_g * up_pre).astype(BF16)
    slope[...] = up_pre * sigmoid_g * (1.0 + gate_pre * (1.0 - sigmoid_g))
    silu[...] = silu_g


def token_rows(parts):
    return jnp.concatenate([p[:p.shape[0] // 2, :] for p in parts], axis=0)


def scaled_rows(parts):
    return jnp.concatenate([p[p.shape[0] // 2:, :] for p in parts], axis=0)


def forward_first_kernel(me, part, *refs, cols):
    pieces, (hidden, slope, silu, gate_w, up_w) = refs[:-5], refs[-5:]
    rows = pieces[0].shape[0]
    half = pieces[0].shape[1] // 2
    for piece, place in zip(pieces, piece_places(me[0], cols)):
        at = pl.ds(pl.multiple_of(place * rows, rows), rows)
        gate_w[at, :] = piece[:, :half]
        up_w[at, :] = piece[:, half:]
    forward_math(token_rows([part]), gate_w[...], up_w[...], hidden, slope, silu)


def forward_kernel(part, gate_w, up_w, hidden, slope, silu):
    forward_math(token_rows([part]), gate_w[...], up_w[...], hidden, slope, silu)


def down_kernel(me, *refs, cols):
    pieces, down_w = refs[:-1], refs[-1]
    rows = pieces[0].shape[0]
    for k, piece in enumerate(pieces):
        there = (me[0] % cols + cols - k) % cols
        down_w[pl.ds(pl.multiple_of(there * rows, rows), rows), :] = piece[...]


def backward_kernel(gate_w, up_w, down_w, *refs):
    n = len(refs) // 4
    hidden, slope, silu = (
        jnp.concatenate([r[...] for r in refs[k * n:(k + 1) * n]], axis=0) for k in range(3)
    )
    parts, back = refs[3 * n:4 * n], refs[-1]
    hidden_back = dot(scaled_rows(parts), down_w[...], (1, 1))
    slot_sums = jnp.sum(hidden.astype(F32) * hidden_back, axis=1, keepdims=True)
    grad_gate = (hidden_back * slope).astype(BF16)
    grad_up = (hidden_back * silu).astype(BF16)
    rows = hidden_back.shape[0]
    width = gate_w.shape[0]
    back[:rows, :width] = (
        dot(grad_gate, gate_w[...], (1, 1)) + dot(grad_up, up_w[...], (1, 1))
    ).astype(back.dtype)
    if back.dtype == F32:
        back[:, width:] = gate_lanes(slot_sums, F32)
    else:
        line = to_row(slot_sums)
        top = line.astype(BF16).astype(F32)
        place = lax.broadcasted_iota(jnp.int32, (GATE_ROWS, rows), 0)
        back[rows:, :] = jnp.zeros((GATE_ROWS, width), BF16)
        back[rows:, :rows] = jnp.where(
            place == 0, top, jnp.where(place == 1, line - top, 0.0)
        ).astype(BF16)


def gate_lanes(column, kind):
    column = jnp.broadcast_to(column, (column.shape[0], LANES))
    lane = lax.broadcasted_iota(jnp.int32, column.shape, 1)
    top = column.astype(kind).astype(F32)
    return jnp.where(lane == 0, top, jnp.where(lane == 1, column - top, 0.0)).astype(kind)


def merge_kernel(own, came, *blocks):
    tall = own.shape[0]
    rows, width = tall // len(blocks), own.shape[1] - LANES
    came_gates = to_column(jnp.sum(came[tall:, :tall].astype(F32), axis=0, keepdims=True))
    strip = blocks[0].shape[0]
    for k, block in enumerate(blocks):
        for j in range(rows // strip):
            at = slice(k * rows + j * strip, k * rows + (j + 1) * strip)
            block[:, j * width:(j + 1) * width] = (own[at, :width] + came[at, :].astype(F32)).astype(BF16)
        at = slice(k * rows, (k + 1) * rows)
        line = to_row(jnp.sum(own[at, width:], axis=1, keepdims=True) + came_gates[at, :])
        top = line.astype(BF16).astype(F32)
        place = lax.broadcasted_iota(jnp.int32, (strip, rows), 0)
        start = rows // strip * width
        block[:, start:] = jnp.zeros((strip, LANES), BF16)
        block[:, start:start + rows] = jnp.where(
            place == 0, top, jnp.where(place == 1, line - top, 0.0)
        ).astype(BF16)


def weight_kernel(me, *refs, cols, n_hidden):
    hiddens, parts, (kept, sent, term) = refs[:n_hidden], refs[n_hidden:-3], refs[-3:]
    hidden = jnp.concatenate([h[...] for h in hiddens], axis=0)
    term[...] = dot(hidden, scaled_rows(parts), (0, 0))
    rows = kept.shape[0]
    col = me[0] % cols
    kept[...] = term[pl.ds(pl.multiple_of(col * rows, rows), rows), :]
    for k in range(1, cols):
        there = (col + k) % cols
        sent[k - 1] = term[pl.ds(pl.multiple_of(there * rows, rows), rows), :].astype(BF16)


def return_kernel(dest, prob, *refs):
    blocks, (d_tokens, d_gate) = refs[:-2], refs[-2:]
    per_dev, width = d_tokens.shape
    strip = blocks[0].shape[0]
    n = (blocks[0].shape[1] - LANES) // width
    rows = n * strip
    dest_col = to_column(dest[...])
    strips, total = [], jnp.zeros((per_dev, 1), F32)
    for k, block in enumerate(blocks):
        strips += [block[:, j * width:(j + 1) * width] for j in range(n)]
        line = jnp.sum(block[:, n * width:n * width + rows].astype(F32), axis=0, keepdims=True)
        here = lax.broadcasted_iota(jnp.int32, (per_dev, rows), 1) + k * rows == dest_col
        total = total + jnp.sum(
            jnp.where(here, jnp.broadcast_to(line, (per_dev, rows)), 0.0), axis=1, keepdims=True
        )
    back = jnp.concatenate(strips, axis=0)
    pick = jnp.where(
        lax.broadcasted_iota(jnp.int32, (back.shape[0], per_dev), 0) == dest[...], 1.0, 0.0
    ).astype(BF16)
    d_tokens[...] = dot(pick, back, (0, 0)).astype(BF16)
    d_gate[...] = to_row(total) / prob[...]


def body(tokens, cotangent, gate_prob, bin_ids, w_gate, w_up, w_down):
    experts = lax.axis_size("expert")
    dp = lax.axis_size("dp")
    cols = dp // 2
    per_dev, width = tokens.shape
    ff = w_gate.shape[2]
    half = ff // 2
    gate_rows = w_gate.shape[1]
    down_rows = w_down.shape[1]
    capacity = 3 * per_dev // experts
    slots = experts * capacity
    strip = 8 if capacity % 8 == 0 else capacity
    here = experts // 2
    me = lax.axis_index("dp").astype(jnp.int32).reshape(1)
    my_expert = lax.axis_index("expert").astype(jnp.int32).reshape(1)

    def after(value, *done):
        return lax.optimization_barrier((value,) + done)[0]

    def over_rows(value):
        return lax.ppermute(value, "dp", [(i, (i + cols) % dp) for i in range(dp)])

    def over_cols(value, k):
        return lax.ppermute(
            value, "dp", [(i, i // cols * cols + (i + k) % cols) for i in range(dp)]
        )

    def flipped(value, k):
        return lax.ppermute(value, "expert", [(i, i ^ k) for i in range(experts)])

    shifts = range(1, cols)
    prob_row = gate_prob.reshape(1, per_dev)
    mine, other = call(
        functools.partial(halves_kernel, cols=cols), 1, 2,
        (like((gate_rows, ff), BF16), like((gate_rows, ff), BF16)),
        [pltpu.VMEM((2, gate_rows, ff), BF16), pltpu.SemaphoreType.DMA((2,))],
        pl.BlockSpec(memory_space=pl.ANY),
    )(me, *[pltpu.with_memory_space_constraint(w[0], pltpu.HBM) for w in (w_gate, w_up)])
    dest, *blocks = call(
        dispatch_kernel, 1, 4,
        (like((1, per_dev), jnp.int32),) + (like((2 * capacity, width), BF16),) * experts,
        spec=pl.BlockSpec(),
    )(after(my_expert, mine), bin_ids.reshape(1, per_dev), prob_row, tokens, cotangent)

    across = over_rows(other)
    beside = [over_cols(mine, k) for k in shifts]
    came = {0: blocks[0]}

    def fetch(k, *done):
        came[k] = flipped(after(blocks[k], *done) if done else blocks[k], k)

    fetch(here)
    for k in range(2, here):
        fetch(k, *([came[k - 2]] if k >= 4 else []))
    fetch(here + 1, came[2])
    fetch(1, came[2], came[here])
    for k in range(here + 2, experts):
        fetch(k, came[k - 2])

    def group(flips):
        return call(group_kernel, 0, len(flips), like((2 * capacity * len(flips), width), BF16))(
            *[came[k] for k in flips]
        )

    middle = here + 3 * (here // 4)
    spans = (range(here), range(here, middle), range(middle, experts))
    parts0 = [group(span) for span in spans[:2]]
    near1 = over_rows(after(parts0[0], across))
    mid1 = over_rows(after(parts0[1], near1, came[experts - 2]))
    relayed = [over_cols(after(across, beside), k) for k in shifts]
    down_own = after(w_down[0], relayed, near1)
    downs = [down_own] + [over_cols(down_own, k) for k in shifts]
    pieces = [mine, across] + [v for pair in zip(beside, relayed) for v in pair]

    def acts(rows):
        return (like((rows, half), BF16), like((rows, half), F32), like((rows, half), F32))

    def tall(part):
        return part.shape[0] // 2

    whole = like((width, half), BF16)
    *first, gate_w, up_w = call(
        functools.partial(forward_first_kernel, cols=cols), 1, 1 + dp,
        acts(tall(parts0[0])) + (whole, whole),
    )(me, parts0[0], *pieces)
    down_w = call(
        functools.partial(down_kernel, cols=cols), 1, cols, like((half, width), BF16)
    )(me, *downs)

    def forward(part):
        return call(forward_kernel, 0, 3, acts(tall(part)))(part, gate_w, up_w)

    def backward(values, parts, kind, *done):
        rows = sum(tall(part) for part in parts)
        return call(
            backward_kernel, 0, 3 + 4 * len(parts),
            like((rows, width + LANES) if kind == F32 else (rows + GATE_ROWS, width), kind),
        )(after(gate_w, *done), up_w, down_w, *[v for each in zip(*values) for v in each], *parts)

    def merge(own, came, n):
        block = like((strip, capacity // strip * width + LANES), BF16)
        return call(merge_kernel, 0, 2, (block,) * n)(own, came)

    near0, mid0 = parts0
    acts0 = [first, forward(mid0)]
    acts1 = [forward(near1)]
    early = [values[0] for values in acts0 + acts1]
    came[experts - 1] = after(came[experts - 1], *early)
    last0 = group(spans[2])
    last1 = over_rows(after(last0, near1))
    parts0.append(last0)
    acts0.append(forward(last0))
    acts1.append(forward(mid1))
    ready = [values[0] for values in acts0 + acts1]
    back_mid1 = backward([acts1[1]], [mid1], BF16, *ready)
    back_mid0 = backward([acts0[1]], [mid0], F32, back_mid1)
    last1 = after(last1, back_mid0)
    came_mid = over_rows(after(back_mid1, last1))
    acts1.append(forward(last1))
    back_rest1 = backward([acts1[2], acts1[0]], [last1, near1], BF16)
    kept, sent = call(
        functools.partial(weight_kernel, cols=cols, n_hidden=6), 1, 12,
        (like((down_rows, width), F32), like((cols - 1, down_rows, width), BF16)),
        [pltpu.VMEM((half, width), F32)],
    )(me, after(acts0[0][0], back_rest1), acts0[1][0], acts0[2][0], *[a[0] for a in acts1],
      near0, mid0, last0, near1, mid1, last1)
    came_rest = over_rows(after(back_rest1, came_mid, kept))
    mid_blocks = merge(after(back_mid0, kept), came_mid, middle - here)
    home = {k: flipped(block, k) for k, block in zip(range(here, middle), mid_blocks)}
    grad_came = [over_cols(sent[k - 1], k) for k in shifts]
    back_rest0 = backward(
        [acts0[2], acts0[0]], [last0, near0], F32, home[here]
    )
    order = [*range(middle, experts), *range(here)]
    rest_blocks = dict(zip(order, merge(after(back_rest0, home[here], home[here + 1]), came_rest, len(order))))
    home[0] = rest_blocks[0]
    for k in [k for k in order if k > 1]:
        home[k] = flipped(rest_blocks[k], k)
    home[1] = flipped(after(rest_blocks[1], home[2], home[middle - 1]), 1)
    d_tokens, d_gate = call(
        return_kernel, 0, 2 + experts, (like((per_dev, width), BF16), like((1, per_dev), F32))
    )(dest, prob_row, *[home[k] for k in range(experts)])
    grad_rows = kept
    for value in grad_came:
        grad_rows = grad_rows + value.astype(F32)
    return (d_tokens, d_gate.reshape(per_dev), grad_rows[None])


def solution(mesh):
    placed = (
        P(("dp", "expert"), None),
        P(("dp", "expert"), None),
        P(("dp", "expert")),
        P(("dp", "expert"), None),
        P("expert", "dp", None),
        P("expert", "dp", None),
        P("expert", "dp", None),
    )
    return jax.shard_map(
        body,
        mesh=mesh,
        in_specs=placed,
        out_specs=(P(("dp", "expert"), None), P(("dp", "expert")), P("expert", "dp", None)),
        check_vma=False,
    )
```
